512 devices in a mesh: dp: 32 (over z, core), expert: 16 (over x, y).
Axes of the slice: x: 4, y: 4, z: 16, core: 2. Of those that a mesh axis runs over, the one named last changes fastest.
Arguments:
- cached_hidden: bfloat16 [65536, 1536], P(('dp', 'expert')), may hold values from -6 to 6
- direction: bfloat16 [16, 2880, 1536], P('expert', 'dp'), may hold values from -1 to 1
- expert_ids: int32 [65536, 4], P(('dp', 'expert')), may hold values from 0 to 127, as said below
- gate_weights: float32 [65536, 4], P(('dp', 'expert')), may hold values from 0.05 to 1
Outputs:
- curvature_product: float32 [16, 2880, 1536], P('expert', 'dp')
The draws below stay inside these ranges and needn't reach their ends.
Inputs may be any that keep to these rules, and one draw needn't show every extreme that they name: `expert_ids`: each row names 4 different experts, at most two of them below 16. Among the 128 rows of one device no expert below 16 is named more than 8 times; for every dp index, some expert below 16 is named exactly 8 times by the rows of each device with that dp index.
All inputs are finite; a program needn't handle non-finite values.
Results may differ from the reference program's by a relative error of at most 0.0034.
Values may be sent and summed in bfloat16 or wider, within the bound.
No kernel may reach another device: no remote copies, remote signals or barrier semaphores. Data moves between devices by JAX's collectives and lax.ppermute only.
A program may use at most 128 MiB of HBM per device.

```python
import math
import jax
import jax.numpy as jnp
from jax import lax

D = 2880
FW = 1536
ALL_EXPERTS = 128
TOPK = 4
T_DEV = 128
EXPERTS = 16
CAP = 8
TOKENS = 65536
N_DP = 32
N_EXPERT = 16


def draw_expert_ids(key, part):
    out_band = (ALL_EXPERTS - EXPERTS) // TOPK

    def one_block(position):
        row_number = position // N_EXPERT
        block_key = jax.random.fold_in(key, position)
        row_key = jax.random.fold_in(key, 7919 * N_DP * N_EXPERT + row_number)
        sub_keys = jax.random.split(block_key, 4)
        full_one = jax.random.randint(row_key, (), 0, EXPERTS)
        counts = jax.random.randint(sub_keys[0], (EXPERTS,), CAP // 4, CAP // 2 + 1)
        counts = jnp.where(jnp.arange(EXPERTS) == full_one, CAP, counts).astype(jnp.int32)
        bounds = jnp.cumsum(counts)
        filled = bounds[-1]
        half_point = jnp.maximum((filled + 1) // 2, CAP)
        order = jax.random.permutation(sub_keys[1], T_DEV).astype(jnp.int32)
        rotate = jax.random.randint(sub_keys[2], (T_DEV,), 0, TOPK)
        outside = EXPERTS + jnp.arange(TOPK)[None, :] * out_band + jax.random.randint(sub_keys[3], (T_DEV, TOPK), 0, out_band)
        columns = []
        for choice_rank in range(TOPK):
            column = (choice_rank - rotate) % TOPK
            pair = order + column * half_point
            limit = jnp.where(column == 0, half_point, filled)
            inner = jnp.sum((bounds[None, :] <= pair[:, None]).astype(jnp.int32), axis=1)
            usable = (column < 2) & (pair < limit)
            columns.append(jnp.where(usable, inner, outside[:, choice_rank]))
        return jnp.stack(columns, axis=1).astype(jnp.int32)
    blocks = jax.vmap(one_block)(jnp.arange(N_DP * N_EXPERT, dtype=jnp.int32))
    return blocks.reshape(N_DP * N_EXPERT * T_DEV, TOPK).astype(jnp.int32)


def block_positions(block_ids):
    flat = block_ids.reshape(-1)
    onehot = (flat[:, None] == jnp.arange(EXPERTS, dtype=jnp.int32)[None, :]).astype(jnp.int32)
    before = jnp.cumsum(onehot, axis=0) - onehot
    return jnp.sum(before * onehot, axis=1).astype(jnp.int32).reshape(block_ids.shape)


def slot_tokens(key, part):
    ids_four = draw_expert_ids(key, part).reshape(N_DP, N_EXPERT, T_DEV, TOPK)
    slot_pos = jax.vmap(jax.vmap(block_positions))(ids_four)
    treated = ids_four < EXPERTS
    owner_index = jnp.where(treated, ids_four, EXPERTS).astype(jnp.int32)
    row_index = jnp.broadcast_to(jnp.arange(N_DP, dtype=jnp.int32)[:, None, None, None], ids_four.shape)
    source_index = jnp.broadcast_to(jnp.arange(N_EXPERT, dtype=jnp.int32)[None, :, None, None], ids_four.shape)
    local_index = jnp.broadcast_to(jnp.arange(T_DEV, dtype=jnp.int32)[None, None, :, None], ids_four.shape)
    token_index = ((row_index * N_EXPERT + source_index) * T_DEV + local_index).astype(jnp.int32)
    table = jnp.full((N_DP, EXPERTS, N_EXPERT, CAP), -1, jnp.int32)
    table = table.at[row_index, owner_index, source_index, slot_pos].set(token_index, mode='drop')
    spare = TOKENS + jnp.arange(N_DP * EXPERTS * N_EXPERT * CAP, dtype=jnp.int32).reshape(table.shape)
    return jnp.where(table >= 0, table, spare).astype(jnp.int32)


def draw_cached_hidden(key, part):
    token_table = slot_tokens(key, part).reshape(N_DP, EXPERTS * N_EXPERT * CAP)
    shared_key = jax.random.fold_in(key, 1000003)
    noise_key = jax.random.fold_in(key, 1000033)

    def shared_row(token):
        row_key = jax.random.fold_in(shared_key, token)
        return jax.random.normal(row_key, (FW,), jnp.float32)

    def one_row_block(inputs):
        row_number, token_list = inputs
        shared = jax.vmap(shared_row)(token_list)
        block_key = jax.random.fold_in(noise_key, row_number)
        noise = jax.random.normal(block_key, (token_list.shape[0], FW), jnp.float32)
        rows = 0.9 * shared + 0.436 * noise
        return jnp.clip(rows, -6.0, 6.0).astype(jnp.bfloat16)
    blocks = lax.map(one_row_block, (jnp.arange(N_DP, dtype=jnp.int32), token_table))
    return blocks.reshape(N_DP * EXPERTS * N_EXPERT * CAP, FW)


def draw_direction(key, part):
    common_key = jax.random.fold_in(key, 2000003)
    own_key = jax.random.fold_in(key, 2000029)
    common = jax.random.normal(common_key, (D, FW), jnp.float32)
    own = jax.random.normal(own_key, (EXPERTS, D, FW), jnp.float32)
    mixed = (0.8 * common[None, :, :] + 0.6 * own) * (1.0 / math.sqrt(FW))
    limit = min(1.0, 6.0 / math.sqrt(FW))
    return jnp.clip(mixed, -limit, limit).astype(jnp.bfloat16)


def block_levels(stream_key, dims, shards, least, largest):
    factor_of = 1.0
    for dim, blocks in shards:
        steps = jax.random.uniform(jax.random.fold_in(jax.random.fold_in(stream_key, 6), dim), (blocks,), jnp.float32, least / len(shards), largest / len(shards))
        factor_of = factor_of * jnp.repeat(jnp.exp(steps), dims[dim] // blocks).reshape((-1,) + (1,) * (len(dims) - 1 - dim))
    return factor_of


def setup_inputs(seed: int = 0) -> dict:
    key_of = jax.random.split(jax.random.key(seed), 5)
    return {
        "cached_hidden": draw_cached_hidden(jax.random.fold_in(key_of[4], 71), 0),
        "direction": draw_direction(jax.random.fold_in(key_of[4], 71), 0),
        "expert_ids": draw_expert_ids(jax.random.fold_in(key_of[4], 71), 0),
        "gate_weights": jnp.clip(jnp.exp(math.log(1.0) - 2.9957323 * jax.random.uniform(key_of[3], (TOKENS, TOPK), jnp.float32) ** block_levels(key_of[3], (TOKENS, TOPK), ((0, 512),), -0.2, 0.2)), 0.05, 1.0),
    }


def slot_positions(block_ids, experts):
    flat = block_ids.reshape(-1)
    onehot = (flat[:, None] == jnp.arange(experts, dtype=jnp.int32)[None, :]).astype(jnp.int32)
    before = jnp.cumsum(onehot, axis=0) - onehot
    return lax.optimization_barrier(jnp.sum(before * onehot, axis=1)).astype(jnp.int32).reshape(block_ids.shape)

def reference(cached_hidden, direction, expert_ids, gate_weights):
    rows_five = cached_hidden.reshape(N_DP, EXPERTS, N_EXPERT, CAP, FW)

    def forward(owner):
        block = rows_five[:, owner].reshape(-1, FW)
        result = lax.dot_general(block, direction[owner], (((1,), (1,)), ((), ())), preferred_element_type=jnp.float32)
        return result.astype(jnp.bfloat16).reshape(N_DP, N_EXPERT, CAP, D)
    tangent = lax.map(forward, jnp.arange(EXPERTS, dtype=jnp.int32))
    ids_four = expert_ids.reshape(N_DP, N_EXPERT, T_DEV, TOPK)
    treated = ids_four < EXPERTS
    safe_ids = jnp.where(treated, ids_four, 0).astype(jnp.int32)
    drop_ids = jnp.where(treated, ids_four, EXPERTS).astype(jnp.int32)
    slot_pos = jax.vmap(jax.vmap(lambda blk: slot_positions(blk, EXPERTS)))(ids_four)
    row_index = jnp.broadcast_to(jnp.arange(N_DP, dtype=jnp.int32)[:, None, None, None], ids_four.shape)
    source_index = jnp.broadcast_to(jnp.arange(N_EXPERT, dtype=jnp.int32)[None, :, None, None], ids_four.shape)
    picked = tangent[safe_ids, row_index, source_index, slot_pos]
    gates_four = jnp.where(treated, gate_weights.reshape(N_DP, N_EXPERT, T_DEV, TOPK), 0.0)
    scale_factor = 1.0 / math.sqrt(TOKENS)
    combined = lax.optimization_barrier(jnp.sum(gates_four[..., None] * picked.astype(jnp.float32), axis=3)) * scale_factor
    outgoing = (gates_four[..., None] * combined[:, :, :, None, :]).astype(jnp.bfloat16)
    adjoint = jnp.zeros((EXPERTS, N_DP, N_EXPERT, CAP, D), jnp.bfloat16)
    adjoint = adjoint.at[drop_ids, row_index, source_index, slot_pos].set(outgoing, mode='drop')

    def backward(owner):
        block = rows_five[:, owner].reshape(-1, FW)
        adj_rows = adjoint[owner].reshape(-1, D)
        return lax.dot_general(adj_rows, block, (((0,), (0,)), ((), ())), preferred_element_type=jnp.float32)
    return lax.map(backward, jnp.arange(EXPERTS, dtype=jnp.int32))
```

```python
import math

import jax
import jax.numpy as jnp
from jax import lax
from jax.sharding import PartitionSpec as P

CHUNKS = 4


def slot_tables(expert_ids, gate_weights, experts, capacity):
    topk = expert_ids.shape[1]
    ids = expert_ids.reshape(-1)
    pairs = ids.shape[0]
    index = jnp.arange(pairs, dtype=jnp.int32)
    onehot = (ids[:, None] == jnp.arange(experts, dtype=jnp.int32)[None, :]).astype(jnp.float32)
    earlier = (index[None, :] < index[:, None]).astype(jnp.bfloat16)
    before = jnp.dot(earlier, onehot.astype(jnp.bfloat16), preferred_element_type=jnp.float32)
    position = jnp.sum(before * onehot, axis=1).astype(jnp.int32)
    slot = jnp.where(ids < experts, ids * capacity + position, -1)
    holds = slot[:, None] == jnp.arange(experts * capacity, dtype=jnp.int32)[None, :]
    token = (index // topk).astype(jnp.float32)
    gates = gate_weights.reshape(-1)
    tokens = jnp.sum(jnp.where(holds, token[:, None], 0.0), axis=0)
    weights = jnp.sum(jnp.where(holds, gates[:, None], 0.0), axis=0)
    return jnp.stack([tokens, weights])


def body(cached_hidden, direction, expert_ids, gate_weights):
    rows = lax.axis_size("dp")
    experts = lax.axis_size("expert")
    capacity = cached_hidden.shape[0] // experts
    tok_count = expert_ids.shape[0]
    scale = 1.0 / math.sqrt(tok_count * rows * experts)
    local_dir = direction[0]
    sources = experts // CHUNKS
    part = sources * capacity
    share = rows // experts
    gathered = [
        lax.all_gather(cached_hidden[j * part : (j + 1) * part], "dp", axis=0, tiled=True)
        for j in range(CHUNKS)
    ]
    tables = slot_tables(expert_ids, gate_weights, experts, capacity)
    tables = jnp.broadcast_to(tables[None], (rows,) + tables.shape)
    tables = lax.all_to_all(tables, "dp", split_axis=0, concat_axis=0, tiled=True)
    tables = lax.all_to_all(tables, "expert", split_axis=0, concat_axis=0, tiled=True)
    tables = tables.reshape(CHUNKS, sources, share, 2, experts, capacity)
    tables = tables.transpose(0, 3, 4, 2, 1, 5)
    block = (
        jnp.arange(share, dtype=jnp.float32)[:, None] * sources
        + jnp.arange(sources, dtype=jnp.float32)[None, :]
    )
    keys = tables[:, 0] + (tok_count * block)[None, None, :, :, None]
    keys = keys.reshape(CHUNKS, -1)
    weights = tables[:, 1].reshape(CHUNKS, -1)
    total = None
    for j in range(CHUNKS):
        same = keys[j][:, None] == keys[j][None, :]
        mix = jnp.where(same, (scale * weights[j])[:, None] * weights[j][None, :], 0.0)
        high = lax.reduce_precision(mix, 8, 7)
        low = (mix - high).astype(jnp.bfloat16)
        high = high.astype(jnp.bfloat16)
        block_rows = gathered[j]
        if total is not None:
            block_rows, total = lax.optimization_barrier((block_rows, total))
        tangent = lax.dot_general(
            block_rows, local_dir, (((1,), (1,)), ((), ())), preferred_element_type=jnp.float32
        ).astype(jnp.bfloat16)
        arrived = lax.all_to_all(tangent, "expert", split_axis=0, concat_axis=0, tiled=True)
        adjoint = jnp.dot(high, arrived, preferred_element_type=jnp.float32) + jnp.dot(
            low, arrived, preferred_element_type=jnp.float32
        )
        adjoint = adjoint.astype(jnp.bfloat16)
        back = lax.all_to_all(adjoint, "expert", split_axis=0, concat_axis=0, tiled=True)
        term = lax.dot_general(
            back, block_rows, (((0,), (0,)), ((), ())), preferred_element_type=jnp.float32
        )
        total = term if total is None else total + term
    return total[None]


def solution(mesh):
    return jax.shard_map(
        body,
        mesh=mesh,
        in_specs=(
            P(("dp", "expert"), None),
            P("expert", "dp", None),
            P(("dp", "expert"), None),
            P(("dp", "expert"), None),
        ),
        out_specs=P("expert", "dp", None),
        check_vma=False,
    )
```

```python
import functools
import math

import jax
import jax.numpy as jnp
from jax import lax
from jax.experimental import pallas as pl
from jax.experimental.pallas import tpu as pltpu
from jax.sharding import PartitionSpec as P

VMEM = pltpu.VMEM
FEATS = 96
TAB = 8


def whole():
    return pl.BlockSpec(memory_space=VMEM)


def table_kernel(capacity, experts, ids_ref, gates_ref, out_ref):
    topk, tokens = ids_ref.shape
    slots = experts * capacity
    slot = lax.broadcasted_iota(jnp.int32, (slots, tokens), 0)
    expert = slot // capacity
    place = (slot % capacity).astype(jnp.float32)
    named = [ids_ref[k : k + 1, :] == expert for k in range(topk)]
    any_named = functools.reduce(jnp.logical_or, named)
    first = lax.broadcasted_iota(jnp.int32, (tokens, tokens), 0)
    second = lax.broadcasted_iota(jnp.int32, (tokens, tokens), 1)
    earlier = (first < second).astype(jnp.float32).astype(jnp.bfloat16)
    before = jnp.dot(
        any_named.astype(jnp.float32).astype(jnp.bfloat16),
        earlier,
        preferred_element_type=jnp.float32,
    )
    here = before == place
    token = lax.broadcasted_iota(jnp.int32, (1, tokens), 1).astype(jnp.float32)
    total = jnp.zeros((8, slots), jnp.float32)
    for k in range(topk):
        gate = gates_ref[k : k + 1, :]
        high = gate.astype(jnp.bfloat16).astype(jnp.float32)
        middle = (gate - high).astype(jnp.bfloat16).astype(jnp.float32)
        low = gate - high - middle
        rows = jnp.concatenate(
            [token, high, middle, low, jnp.zeros((4, tokens), jnp.float32)], axis=0
        ).astype(jnp.bfloat16)
        holds = jnp.logical_and(named[k], here).astype(jnp.float32).astype(jnp.bfloat16)
        total += lax.dot_general(
            rows, holds, (((1,), (1,)), ((), ())), preferred_element_type=jnp.float32
        )
    out_ref[...] = jnp.zeros(out_ref.shape, out_ref.dtype)
    out_ref[:, :slots] = total.astype(out_ref.dtype)


def slot_table(ids, gates, experts, capacity, width):
    return pl.pallas_call(
        functools.partial(table_kernel, capacity, experts),
        out_shape=jax.ShapeDtypeStruct((TAB, width), jnp.bfloat16),
        in_specs=[whole(), whole()],
        out_specs=whole(),
        name="slot_table",
    )(ids.T, gates.T)


def tangent_kernel(rows_a, rows_b, dir_ref, _, out_ref):
    sources = out_ref.shape[0]
    span = sources * out_ref.shape[2]
    tails = []
    for i, rows in enumerate((rows_a, rows_b)):
        value = jnp.dot(rows[:span, :], dir_ref[...], preferred_element_type=jnp.float32)
        out_ref[:, i] = value[:, :128].reshape(sources, -1, 128).astype(jnp.bfloat16)
        tails.append(value[:, 128:])
    tail = jnp.concatenate(tails, axis=1)
    out_ref[:, 2] = tail.reshape(sources, -1, 128).astype(jnp.bfloat16)


def tangents(pair, rows_a, rows_b, dirs, packed, shape):
    sources, slabs, capacity, _ = shape
    flops = 2 * 2 * sources * capacity * dirs.shape[0] * dirs.shape[1]
    args = [rows_a, rows_b, dirs] + ([] if packed is None else [packed])

    def kernel(a, b, d, *rest):
        tangent_kernel(a, b, d, None, rest[-1])

    return pl.pallas_call(
        kernel,
        grid=(1,),
        out_shape=jax.ShapeDtypeStruct(shape, jnp.bfloat16),
        in_specs=[
            pl.BlockSpec(rows_a.shape, lambda i: (0, 0)),
            pl.BlockSpec(rows_b.shape, lambda i: (0, 0)),
            pl.BlockSpec(dirs.shape, lambda i: (0, 0)),
        ]
        + ([] if packed is None else [pl.BlockSpec(memory_space=pl.ANY)]),
        out_specs=pl.BlockSpec((sources, 3, capacity, 128), lambda i: (0, pair, 0, 0)),
        input_output_aliases={} if packed is None else {3: 0},
        cost_estimate=pl.CostEstimate(
            flops=flops, bytes_accessed=2 * rows_a.size * 2 + dirs.size * 2, transcendentals=0
        ),
        name="tangents",
    )(*args)


def combine_kernel(scale, in_ref, *refs):
    tables, out_ref = refs[:-1], refs[-1]
    experts, slabs, capacity, _ = in_ref.shape
    slots = experts * capacity
    lane = lax.broadcasted_iota(jnp.int32, (slots, 128), 1)

    def mix_of(table):
        rows = table.astype(jnp.float32)
        gate = rows[1:2] + rows[2:3] + rows[3:4]
        both = jnp.concatenate([rows[0:1], gate, jnp.zeros((6, slots), jnp.float32)], axis=0)
        columns = both.T
        mix = jnp.where(
            columns[:, 0:1] == both[0:1], (scale * columns[:, 1:2]) * both[1:2], 0.0
        )
        high = mix.astype(jnp.bfloat16)
        return high, (mix - high.astype(jnp.float32)).astype(jnp.bfloat16)

    def apply(mix, x):
        return jnp.dot(mix[0], x, preferred_element_type=jnp.float32) + jnp.dot(
            mix[1], x, preferred_element_type=jnp.float32
        )

    def load(slab):
        return in_ref[:, slab].astype(jnp.float32).reshape(slots, 128).astype(jnp.bfloat16)

    def store(slab, value):
        out_ref[:, slab] = value.reshape(experts, capacity, 128).astype(jnp.bfloat16)

    for pair in range(slabs // 3):
        mixes = [mix_of(tables[2 * pair + i][...]) for i in range(2)]
        for i in range(2):
            store(3 * pair + i, apply(mixes[i], load(3 * pair + i)))
        tail = load(3 * pair + 2)
        store(
            3 * pair + 2,
            jnp.where(lane < 64, apply(mixes[0], tail), apply(mixes[1], tail)),
        )


def combine(packed, tables, scale):
    return pl.pallas_call(
        functools.partial(combine_kernel, scale),
        out_shape=jax.ShapeDtypeStruct(packed.shape, packed.dtype),
        in_specs=[whole()] * (1 + len(tables)),
        out_specs=whole(),
        name="combine",
    )(packed, *tables)


def gradient_kernel(in_ref, *refs):
    blocks, out_ref = refs[:-1], refs[-1]
    sources, slabs, capacity, _ = in_ref.shape
    span = sources * capacity
    pairs = slabs // 3

    def load(slab):
        return in_ref[:, slab].astype(jnp.float32).reshape(span, 128)

    lhs = []
    for pair in range(pairs):
        main = jnp.concatenate([load(3 * pair).T, load(3 * pair + 1).T], axis=1)
        tail = load(3 * pair + 2).T
        tail = jnp.concatenate([tail[:64], tail[64:]], axis=1)
        lhs.append(jnp.concatenate([main, tail], axis=0).astype(jnp.bfloat16))
    width = out_ref.shape[1]
    step = 256
    for start in range(0, width, step):
        total = None
        for pair in range(pairs):
            rhs = jnp.concatenate(
                [blocks[2 * pair + i][:span, start : start + step] for i in range(2)], axis=0
            )
            term = jnp.dot(lhs[pair], rhs, preferred_element_type=jnp.float32)
            total = term if total is None else total + term
        out_ref[:, start : start + step] = total


def gradients(packed, blocks):
    return pl.pallas_call(
        gradient_kernel,
        out_shape=jax.ShapeDtypeStruct((2 * FEATS, blocks[0].shape[1]), jnp.float32),
        in_specs=[whole()] * (1 + len(blocks)),
        out_specs=whole(),
        name="gradients",
    )(packed, *blocks)


def body(cached_hidden, direction, expert_ids, gate_weights):
    rows = lax.axis_size("dp")
    experts = lax.axis_size("expert")
    span, width = cached_hidden.shape
    capacity = span // experts
    feats = direction.shape[1]
    scale = 1.0 / math.sqrt(expert_ids.shape[0] * rows * experts)
    steps = rows // 4
    ring = [(i, (i + 2) % rows if i % 2 == 0 else (i - 2) % rows) for i in range(rows)]
    partner = [(i, i ^ 1) for i in range(rows)]

    def shift(x):
        return lax.ppermute(x, "dp", ring)

    def swap(x):
        return lax.ppermute(x, "dp", partner)

    first = shift(cached_hidden)
    own_table = slot_table(expert_ids, gate_weights, experts, capacity, width)
    sent = jnp.concatenate([cached_hidden, own_table], axis=0)
    other = swap(sent)
    chip_table = jnp.concatenate(
        [own_table[:, :128], other[span:, :128], jnp.zeros((TAB, width - 256), jnp.bfloat16)], axis=1
    )
    message = jnp.concatenate([other[:span], chip_table], axis=0)
    other_dir = swap(direction[0])
    pad = jnp.zeros((FEATS - feats, width), jnp.bfloat16)
    dirs = jnp.concatenate([direction[0], pad, other_dir, pad], axis=0).T
    chain_a = [first]
    chain_b = [shift(message)]
    for _ in range(1, steps - 1):
        chain_a.append(shift(chain_a[-1]))
        chain_b.append(shift(chain_b[-1]))
    chain_a.append(shift(chain_a[-1]))
    last_table = shift(chain_b[-1][span:])
    pairs = [(chain_a[s], chain_b[s]) for s in range(steps - 1)] + [(cached_hidden, chain_a[-1])]
    tables = []
    for s in range(steps - 1):
        chip = chain_b[s][span:]
        tables += [chip[:, :128], chip[:, 128:256]]
    tables += [own_table[:, :128], last_table[:, :128]]
    shape = (experts, 3 * steps, capacity, 128)
    packed = None
    for i, (a, b) in enumerate(pairs):
        packed = tangents(i, a, b, dirs, packed, shape)
    arrived = lax.all_to_all(packed, "expert", split_axis=0, concat_axis=0, tiled=True)
    adjoint = combine(arrived, tables, scale)
    back = lax.all_to_all(adjoint, "expert", split_axis=0, concat_axis=0, tiled=True)
    grad = gradients(back, [x for pair in pairs for x in pair])
    theirs = swap(grad[FEATS : FEATS + feats])
    return (grad[:feats] + theirs)[None]


def solution(mesh):
    return jax.shard_map(
        body,
        mesh=mesh,
        in_specs=(
            P(("dp", "expert"), None),
            P("expert", "dp", None),
            P(("dp", "expert"), None),
            P(("dp", "expert"), None),
        ),
        out_specs=P("expert", "dp", None),
        check_vma=False,
    )
```

```python
import functools
import math

import jax
import jax.numpy as jnp
from jax import lax
from jax.experimental import pallas as pl
from jax.experimental.pallas import tpu as pltpu
from jax.sharding import PartitionSpec as P


VMEM = pltpu.VMEM
FEATS = 96
TAB = 8
LANES = 128
LIMIT = 24 * 2**20


def whole():
    return pl.BlockSpec(memory_space=VMEM)


def full(x):
    return pl.BlockSpec(x.shape, lambda i: (0,) * x.ndim)


def params():
    return pltpu.CompilerParams(vmem_limit_bytes=LIMIT)


def cost(flops, nbytes):
    return pl.CostEstimate(flops=flops, bytes_accessed=nbytes, transcendentals=0)


def table_kernel(capacity, experts, ids_ref, gates_ref, out_ref):
    topk, tokens = ids_ref.shape
    slots = experts * capacity
    slot = lax.broadcasted_iota(jnp.int32, (slots, tokens), 0)
    expert = slot // capacity
    place = (slot % capacity).astype(jnp.float32)
    named = [ids_ref[k : k + 1, :] == expert for k in range(topk)]
    any_named = functools.reduce(jnp.logical_or, named)
    first = lax.broadcasted_iota(jnp.int32, (tokens, tokens), 0)
    second = lax.broadcasted_iota(jnp.int32, (tokens, tokens), 1)
    earlier = (first < second).astype(jnp.float32).astype(jnp.bfloat16)
    before = jnp.dot(
        any_named.astype(jnp.float32).astype(jnp.bfloat16),
        earlier,
        preferred_element_type=jnp.float32,
    )
    here = before == place
    token = lax.broadcasted_iota(jnp.int32, (1, tokens), 1).astype(jnp.float32)
    total = jnp.zeros((8, slots), jnp.float32)
    for k in range(topk):
        gate = gates_ref[k : k + 1, :]
        high = gate.astype(jnp.bfloat16).astype(jnp.float32)
        middle = (gate - high).astype(jnp.bfloat16).astype(jnp.float32)
        low = gate - high - middle
        rows = jnp.concatenate(
            [token, high, middle, low, jnp.zeros((4, tokens), jnp.float32)], axis=0
        ).astype(jnp.bfloat16)
        holds = jnp.logical_and(named[k], here).astype(jnp.float32).astype(jnp.bfloat16)
        total += lax.dot_general(
            rows, holds, (((1,), (1,)), ((), ())), preferred_element_type=jnp.float32
        )
    out_ref[...] = total.astype(out_ref.dtype)


def slot_table(ids, gates, experts, capacity):
    return pl.pallas_call(
        functools.partial(table_kernel, capacity, experts),
        out_shape=jax.ShapeDtypeStruct((TAB, experts * capacity), jnp.bfloat16),
        in_specs=[whole(), whole()],
        out_specs=whole(),
        compiler_params=params(),
        cost_estimate=cost(10**7, 10**5),
        name="slot_table",
    )(ids.T, gates.T)


def mix_of(table, scale):
    rows = table.astype(jnp.float32)
    slots = rows.shape[1]
    gate = rows[1:2] + rows[2:3] + rows[3:4]
    both = jnp.concatenate([rows[0:1], gate, jnp.zeros((6, slots), jnp.float32)], axis=0)
    columns = both.T
    mix = jnp.where(columns[:, 0:1] == both[0:1], (scale * columns[:, 1:2]) * both[1:2], 0.0)
    high = mix.astype(jnp.bfloat16)
    low = (mix - high.astype(jnp.float32)).astype(jnp.bfloat16)
    return jnp.concatenate([high, low], axis=1)


def project(rows, dirs):
    return lax.dot_general(
        rows, dirs, (((1,), (1,)), ((), ())), preferred_element_type=jnp.float32
    )


def pack(out_ref, values):
    sources = out_ref.shape[0]
    tail = jnp.concatenate([value[:, LANES:] for value in values], axis=1)
    for i, value in enumerate([value[:, :LANES] for value in values] + [tail]):
        out_ref[:, i] = value.reshape(sources, -1, LANES).astype(jnp.bfloat16)


def tangents(pair, pieces, dirs, kept, shape, mix_shape, scale):
    sources, _, capacity, _ = shape
    span = sources * capacity
    spare = pieces[-1].shape[0] - TAB
    n = len(pieces)
    args = list(pieces) + [pieces[-1], dirs] + list(kept)

    def kernel(*refs):
        table_ref, dir_ref = refs[n], refs[n + 1]
        out_ref, mix_ref = refs[-2], refs[-1]
        parts = [refs[i][...] for i in range(n - 1)] + [refs[n - 1][:spare, :]]
        value = project(jnp.concatenate(parts, axis=0), dir_ref[...])
        pack(out_ref, [value[:span], value[span:]])
        for i in range(2):
            mix_ref[i] = mix_of(table_ref[:, i * LANES : (i + 1) * LANES], scale)

    return pl.pallas_call(
        kernel,
        grid=(1,),
        out_shape=[
            jax.ShapeDtypeStruct(shape, jnp.bfloat16),
            jax.ShapeDtypeStruct(mix_shape, jnp.bfloat16),
        ],
        in_specs=[full(x) for x in pieces]
        + [pl.BlockSpec((TAB, 2 * LANES), lambda i: (spare // TAB, 0)), full(dirs)]
        + [pl.BlockSpec(memory_space=pl.ANY)] * len(kept),
        out_specs=[
            pl.BlockSpec((sources, 3, capacity, LANES), lambda i: (0, pair, 0, 0)),
            pl.BlockSpec((2,) + mix_shape[1:], lambda i: (pair, 0, 0)),
        ],
        input_output_aliases={n + 2 + i: i for i in range(len(kept))},
        compiler_params=params(),
        cost_estimate=cost(4 * span * dirs.size, 2 * 2 * span * dirs.shape[1] + 2 * dirs.size),
        name="tangents",
    )(*args)


def own_tangents(rows, dirs):
    def kernel(rows_ref, dir_ref, out_ref):
        out_ref[...] = project(rows_ref[...], dir_ref[...])

    return pl.pallas_call(
        kernel,
        out_shape=jax.ShapeDtypeStruct((rows.shape[0], dirs.shape[0]), jnp.float32),
        in_specs=[whole(), whole()],
        out_specs=whole(),
        compiler_params=params(),
        cost_estimate=cost(2 * rows.shape[0] * dirs.size, 2 * rows.size + 2 * dirs.size),
        name="own_tangents",
    )(rows, dirs)


def last_tangents(pair, own, rows, dirs, packed):
    sources, _, capacity, _ = packed.shape

    def kernel(own_ref, rows_ref, dir_ref, _, out_ref):
        pack(out_ref, [own_ref[...], project(rows_ref[...], dir_ref[...])])

    return pl.pallas_call(
        kernel,
        grid=(1,),
        out_shape=jax.ShapeDtypeStruct(packed.shape, packed.dtype),
        in_specs=[full(x) for x in (own, rows, dirs)] + [pl.BlockSpec(memory_space=pl.ANY)],
        out_specs=pl.BlockSpec((sources, 3, capacity, LANES), lambda i: (0, pair, 0, 0)),
        input_output_aliases={3: 0},
        compiler_params=params(),
        cost_estimate=cost(2 * own.shape[0] * dirs.size, 2 * dirs.size),
        name="last_tangents",
    )(own, rows, dirs, packed)


def combine(packed, mixes, tables, scale):
    experts, slabs, capacity, _ = packed.shape
    slots = experts * capacity

    def kernel(in_ref, mix_ref, *refs):
        out_ref = refs[-1]
        lane = lax.broadcasted_iota(jnp.int32, (slots, LANES), 1)

        def load(slab):
            return in_ref[:, slab].astype(jnp.float32).reshape(slots, LANES).astype(jnp.bfloat16)

        for pair in range(slabs // 3):
            tail = load(3 * pair + 2)
            tails = []
            for i in range(2):
                x = jnp.concatenate([load(3 * pair + i), tail], axis=1)
                here = 2 * pair + i
                if here < mixes.shape[0]:
                    mix = mix_ref[here]
                else:
                    mix = mix_of(refs[i][...], scale)
                y = jnp.dot(
                    mix, jnp.concatenate([x, x], axis=0), preferred_element_type=jnp.float32
                )
                tails.append(y[:, LANES:])
                out_ref[:, 3 * pair + i] = (
                    y[:, :LANES].reshape(experts, capacity, LANES).astype(jnp.bfloat16)
                )
            both = jnp.where(lane < LANES // 2, tails[0], tails[1])
            out_ref[:, 3 * pair + 2] = both.reshape(experts, capacity, LANES).astype(jnp.bfloat16)

    return pl.pallas_call(
        kernel,
        out_shape=jax.ShapeDtypeStruct(packed.shape, packed.dtype),
        in_specs=[whole()] * (2 + len(tables)),
        out_specs=whole(),
        compiler_params=params(),
        cost_estimate=cost(10**9, 4 * packed.size),
        name="combine",
    )(packed, mixes, *tables)


def gradients(packed, groups, feats):
    sources, slabs, capacity, _ = packed.shape
    span = sources * capacity
    pairs = slabs // 3
    width = groups[0][0].shape[1]
    tiles = width // LANES
    step = 2 * LANES
    pieces = [x for group in groups for x in group]

    def kernel(in_ref, *refs):
        own_ref, other_ref, lhs_ref = refs[-3:]
        column = pl.program_id(0)

        @pl.when(column == 0)
        def _():
            def load(slab):
                return in_ref[:, slab].astype(jnp.float32).reshape(span, LANES)

            for pair in range(pairs):
                main = jnp.concatenate([load(3 * pair).T, load(3 * pair + 1).T], axis=1)
                tail = load(3 * pair + 2).T
                tail = jnp.concatenate([tail[: LANES // 2], tail[LANES // 2 :]], axis=1)
                lhs_ref[pair] = jnp.concatenate([main, tail], axis=0).astype(jnp.bfloat16)

        total = None
        at = 0
        for pair, group in enumerate(groups):
            parts = []
            left = 2 * span
            for piece in group:
                rows = min(left, piece.shape[0])
                parts.append(refs[at][:rows, :])
                left -= rows
                at += 1
            term = jnp.dot(
                lhs_ref[pair], jnp.concatenate(parts, axis=0), preferred_element_type=jnp.float32
            )
            total = term if total is None else total + term
        for i in range(2):
            lanes = slice(i * LANES, (i + 1) * LANES)
            rows = pl.ds(2 * column + i, feats, stride=tiles)
            own_ref[rows, :] = total[:feats, lanes]
            other_ref[rows, :] = total[FEATS : FEATS + feats, lanes]

    shape = jax.ShapeDtypeStruct((feats * tiles, LANES), jnp.float32)
    return pl.pallas_call(
        kernel,
        grid=(width // step,),
        out_shape=[shape, shape],
        in_specs=[full(packed)]
        + [pl.BlockSpec((x.shape[0], step), lambda i: (0, i)) for x in pieces],
        out_specs=[pl.BlockSpec(shape.shape, lambda i: (0, 0))] * 2,
        scratch_shapes=[pltpu.VMEM((pairs, 2 * FEATS, 2 * span), jnp.bfloat16)],
        compiler_params=params(),
        cost_estimate=cost(4 * FEATS * 2 * span * pairs * width, 2 * 2 * span * pairs * width),
        name="gradients",
    )(packed, *pieces)


def body(cached_hidden, direction, expert_ids, gate_weights):
    rows = lax.axis_size("dp")
    experts = lax.axis_size("expert")
    span, width = cached_hidden.shape
    capacity = span // experts
    feats = direction.shape[1]
    scale = 1.0 / math.sqrt(expert_ids.shape[0] * rows * experts)
    steps = rows // 4
    ring = [(i, (i + 2) % rows if i % 2 == 0 else (i - 2) % rows) for i in range(rows)]
    partner = [(i, i ^ 1) for i in range(rows)]

    def shift(x):
        return lax.ppermute(x, "dp", ring)

    def swap(x):
        return lax.ppermute(x, "dp", partner)

    chain_a = [shift(cached_hidden)]
    other = swap(cached_hidden)
    table = slot_table(expert_ids, gate_weights, experts, capacity)
    other_table = swap(table)
    chip_table = jnp.concatenate(
        [table, other_table, jnp.zeros((TAB, width - 2 * span), jnp.bfloat16)], axis=1
    )
    chain_b = [shift(jnp.concatenate([other, chip_table], axis=0))]
    other_dir = swap(direction[0])
    pad = jnp.zeros((FEATS - feats, width), jnp.bfloat16)
    dirs = jnp.concatenate([direction[0], pad, other_dir, pad], axis=0)
    for _ in range(2, steps):
        chain_a.append(shift(chain_a[-1]))
        chain_b.append(shift(chain_b[-1]))
    last = shift(chain_a[-1])
    last_table = shift(chain_b[-1][span:, :LANES])
    shape = (experts, 3 * steps, capacity, LANES)
    mix_shape = (2 * (steps - 1), span, 2 * span)
    kept = ()
    groups = []
    for s in range(1, steps):
        pieces = [chain_a[s - 1], chain_b[s - 1]]
        kept = tangents(s - 1, pieces, dirs, kept, shape, mix_shape, scale)
        groups.append(pieces)
    packed, mixes = kept
    own = own_tangents(cached_hidden, dirs)
    packed = last_tangents(steps - 1, own, last, dirs, packed)
    groups.append([cached_hidden, last])
    arrived = lax.all_to_all(packed, "expert", split_axis=0, concat_axis=0, tiled=True)
    adjoint = combine(arrived, mixes, [table, last_table], scale)
    back = lax.all_to_all(adjoint, "expert", split_axis=0, concat_axis=0, tiled=True)
    mine, theirs = gradients(back, groups, feats)
    theirs = swap(theirs)
    return (mine + theirs).reshape(1, feats, width)


def solution(mesh):
    return jax.shard_map(
        body,
        mesh=mesh,
        in_specs=(
            P(("dp", "expert"), None),
            P("expert", "dp", None),
            P(("dp", "expert"), None),
            P(("dp", "expert"), None),
        ),
        out_specs=P("expert", "dp", None),
        check_vma=False,
    )
```

```python
import functools
import math

import jax
import jax.numpy as jnp
from jax import lax
from jax.experimental import pallas as pl
from jax.experimental.pallas import tpu as pltpu
from jax.sharding import PartitionSpec as P


VMEM = pltpu.VMEM
FEATS = 96
TAB = 8
LANES = 128
LIMIT = 24 * 2**20


def whole():
    return pl.BlockSpec(memory_space=VMEM)


def full(x):
    return pl.BlockSpec(x.shape, lambda i: (0,) * x.ndim)


def params():
    return pltpu.CompilerParams(vmem_limit_bytes=LIMIT)


def cost(flops, nbytes):
    return pl.CostEstimate(flops=flops, bytes_accessed=nbytes, transcendentals=0)


def message_kernel(capacity, experts, rows_hbm, ids_hbm, gates_hbm, out_ref, ids_ref, gates_ref, sems):
    topk, tokens = ids_ref.shape
    slots = experts * capacity
    span, width = rows_hbm.shape
    copies = [
        pltpu.make_async_copy(rows_hbm, out_ref.at[:span], sems.at[0]),
        pltpu.make_async_copy(ids_hbm, ids_ref, sems.at[1]),
        pltpu.make_async_copy(gates_hbm, gates_ref, sems.at[2]),
    ]
    for copy in copies:
        copy.start()
    for copy in copies[1:]:
        copy.wait()
    slot = lax.broadcasted_iota(jnp.int32, (slots, tokens), 0)
    expert = slot // capacity
    place = (slot % capacity).astype(jnp.float32)
    named = [ids_ref[k : k + 1, :] == expert for k in range(topk)]
    any_named = functools.reduce(jnp.logical_or, named)
    first = lax.broadcasted_iota(jnp.int32, (tokens, tokens), 0)
    second = lax.broadcasted_iota(jnp.int32, (tokens, tokens), 1)
    earlier = (first < second).astype(jnp.float32).astype(jnp.bfloat16)
    before = jnp.dot(
        any_named.astype(jnp.float32).astype(jnp.bfloat16),
        earlier,
        preferred_element_type=jnp.float32,
    )
    here = before == place
    token = lax.broadcasted_iota(jnp.int32, (1, tokens), 1).astype(jnp.float32)
    total = jnp.zeros((8, slots), jnp.float32)
    for k in range(topk):
        gate = gates_ref[k : k + 1, :]
        high = gate.astype(jnp.bfloat16).astype(jnp.float32)
        middle = (gate - high).astype(jnp.bfloat16).astype(jnp.float32)
        low = gate - high - middle
        rows = jnp.concatenate(
            [token, high, middle, low, jnp.zeros((4, tokens), jnp.float32)], axis=0
        ).astype(jnp.bfloat16)
        holds = jnp.logical_and(named[k], here).astype(jnp.float32).astype(jnp.bfloat16)
        total += lax.dot_general(
            rows, holds, (((1,), (1,)), ((), ())), preferred_element_type=jnp.float32
        )
    out_ref[span:] = jnp.concatenate(
        [total, jnp.zeros((TAB, width - slots), jnp.float32)], axis=1
    ).astype(out_ref.dtype)
    copies[0].wait()


def message(rows, ids, gates, experts, capacity):
    args = (rows, ids.T, gates.T)
    shape = (rows.shape[0] + TAB, rows.shape[1])
    return pl.pallas_call(
        functools.partial(message_kernel, capacity, experts),
        out_shape=jax.ShapeDtypeStruct(shape, jnp.bfloat16),
        in_specs=[pl.BlockSpec(memory_space=pltpu.HBM)] * 3,
        out_specs=whole(),
        scratch_shapes=[
            pltpu.VMEM(args[1].shape, args[1].dtype),
            pltpu.VMEM(args[2].shape, args[2].dtype),
            pltpu.SemaphoreType.DMA((3,)),
        ],
        cost_estimate=cost(10**7, 10**6),
        name="message",
    )(*args)


def table_of(rows):
    return pl.BlockSpec((TAB, LANES), lambda i: (rows.shape[0] // TAB - 1, 0))


def mix_of(table, scale):
    rows = table.astype(jnp.float32)
    slots = rows.shape[1]
    gate = rows[1:2] + rows[2:3] + rows[3:4]
    both = jnp.concatenate([rows[0:1], gate, jnp.zeros((6, slots), jnp.float32)], axis=0)
    columns = both.T
    mix = jnp.where(columns[:, 0:1] == both[0:1], (scale * columns[:, 1:2]) * both[1:2], 0.0)
    high = mix.astype(jnp.bfloat16)
    low = (mix - high.astype(jnp.float32)).astype(jnp.bfloat16)
    return jnp.concatenate([high, low], axis=1)


def project(rows, dirs):
    return lax.dot_general(
        rows, dirs, (((1,), (1,)), ((), ())), preferred_element_type=jnp.float32
    )


def pack(out_ref, values):
    sources = out_ref.shape[0]
    tail = jnp.concatenate([value[:, LANES:] for value in values], axis=1)
    for i, value in enumerate([value[:, :LANES] for value in values] + [tail]):
        out_ref[:, i] = value.reshape(sources, -1, LANES).astype(jnp.bfloat16)


def tangents(pair, pieces, dirs, kept, shape, mix_shape, scale):
    sources, _, capacity, _ = shape
    span = sources * capacity
    args = list(pieces) + list(pieces) + [dirs] + list(kept)

    def kernel(*refs):
        dir_ref, out_ref, mix_ref = refs[4], refs[-2], refs[-1]
        rows = jnp.concatenate([refs[i][:span, :] for i in range(2)], axis=0)
        value = project(rows, dir_ref[...])
        pack(out_ref, [value[:span], value[span:]])
        for i in range(2):
            mix_ref[i] = mix_of(refs[2 + i][...], scale)

    return pl.pallas_call(
        kernel,
        grid=(1,),
        out_shape=[
            jax.ShapeDtypeStruct(shape, jnp.bfloat16),
            jax.ShapeDtypeStruct(mix_shape, jnp.bfloat16),
        ],
        in_specs=[full(x) for x in pieces]
        + [table_of(x) for x in pieces]
        + [full(dirs)]
        + [pl.BlockSpec(memory_space=pl.ANY)] * len(kept),
        out_specs=[
            pl.BlockSpec((sources, 3, capacity, LANES), lambda i: (0, pair, 0, 0)),
            pl.BlockSpec((2,) + mix_shape[1:], lambda i: (pair, 0, 0)),
        ],
        input_output_aliases={5 + i: i for i in range(len(kept))},
        compiler_params=params(),
        cost_estimate=cost(4 * span * dirs.size, 2 * 2 * span * dirs.shape[1] + 2 * dirs.size),
        name="tangents",
    )(*args)


def own_tangents(rows, dirs):
    def kernel(rows_ref, dir_ref, out_ref):
        out_ref[...] = project(rows_ref[...], dir_ref[...])

    return pl.pallas_call(
        kernel,
        out_shape=jax.ShapeDtypeStruct((rows.shape[0], dirs.shape[0]), jnp.float32),
        in_specs=[whole(), whole()],
        out_specs=whole(),
        compiler_params=params(),
        cost_estimate=cost(2 * rows.shape[0] * dirs.size, 2 * rows.size + 2 * dirs.size),
        name="own_tangents",
    )(rows, dirs)


def last_tangents(pair, own, rows, dirs, packed):
    sources, _, capacity, _ = packed.shape
    span = sources * capacity

    def kernel(own_ref, rows_ref, dir_ref, _, out_ref, held_ref, sem):
        copy = pltpu.make_async_copy(rows_ref, held_ref, sem)
        copy.start()
        copy.wait()
        pack(out_ref, [own_ref[...], project(held_ref[:span, :], dir_ref[...])])

    return pl.pallas_call(
        kernel,
        grid=(1,),
        out_shape=jax.ShapeDtypeStruct(packed.shape, packed.dtype),
        in_specs=[full(own), pl.BlockSpec(memory_space=pltpu.HBM), full(dirs)]
        + [pl.BlockSpec(memory_space=pl.ANY)],
        out_specs=pl.BlockSpec((sources, 3, capacity, LANES), lambda i: (0, pair, 0, 0)),
        scratch_shapes=[pltpu.VMEM(rows.shape, rows.dtype), pltpu.SemaphoreType.DMA],
        input_output_aliases={3: 0},
        compiler_params=params(),
        cost_estimate=cost(2 * own.shape[0] * dirs.size, 2 * dirs.size),
        name="last_tangents",
    )(own, rows, dirs, packed)


def combine(packed, mixes, tables, scale):
    experts, slabs, capacity, _ = packed.shape
    slots = experts * capacity

    def kernel(in_ref, mix_ref, *refs):
        out_ref = refs[-1]
        lane = lax.broadcasted_iota(jnp.int32, (slots, LANES), 1)

        def load(slab):
            return in_ref[:, slab].astype(jnp.float32).reshape(slots, LANES).astype(jnp.bfloat16)

        for pair in range(slabs // 3):
            tail = load(3 * pair + 2)
            tails = []
            for i in range(2):
                x = jnp.concatenate([load(3 * pair + i), tail], axis=1)
                here = 2 * pair + i
                if here < mixes.shape[0]:
                    mix = mix_ref[here]
                else:
                    mix = mix_of(refs[i][...], scale)
                y = jnp.dot(
                    mix, jnp.concatenate([x, x], axis=0), preferred_element_type=jnp.float32
                )
                tails.append(y[:, LANES:])
                out_ref[:, 3 * pair + i] = (
                    y[:, :LANES].reshape(experts, capacity, LANES).astype(jnp.bfloat16)
                )
            both = jnp.where(lane < LANES // 2, tails[0], tails[1])
            out_ref[:, 3 * pair + 2] = both.reshape(experts, capacity, LANES).astype(jnp.bfloat16)

    return pl.pallas_call(
        kernel,
        grid=(1,),
        out_shape=jax.ShapeDtypeStruct(packed.shape, packed.dtype),
        in_specs=[full(packed), full(mixes)] + [table_of(x) for x in tables],
        out_specs=full(packed),
        compiler_params=params(),
        cost_estimate=cost(10**9, 4 * packed.size),
        name="combine",
    )(packed, mixes, *tables)


def gradients(packed, groups, feats):
    sources, slabs, capacity, _ = packed.shape
    span = sources * capacity
    pairs = slabs // 3
    width = groups[0][0].shape[1]
    tiles = width // LANES
    step = 2 * LANES
    pieces = [x for group in groups for x in group]

    def kernel(in_ref, *refs):
        own_ref, other_ref, lhs_ref = refs[-3:]
        column = pl.program_id(0)

        @pl.when(column == 0)
        def _():
            def load(slab):
                return in_ref[:, slab].astype(jnp.float32).reshape(span, LANES)

            for pair in range(pairs):
                main = jnp.concatenate([load(3 * pair).T, load(3 * pair + 1).T], axis=1)
                tail = load(3 * pair + 2).T
                tail = jnp.concatenate([tail[: LANES // 2], tail[LANES // 2 :]], axis=1)
                lhs_ref[pair] = jnp.concatenate([main, tail], axis=0).astype(jnp.bfloat16)

        total = None
        for pair in range(pairs):
            rows = jnp.concatenate([refs[2 * pair + i][:span, :] for i in range(2)], axis=0)
            term = jnp.dot(lhs_ref[pair], rows, preferred_element_type=jnp.float32)
            total = term if total is None else total + term
        for i in range(2):
            lanes = slice(i * LANES, (i + 1) * LANES)
            rows = pl.ds(2 * column + i, feats, stride=tiles)
            own_ref[rows, :] = total[:feats, lanes]
            other_ref[rows, :] = total[FEATS : FEATS + feats, lanes]

    shape = jax.ShapeDtypeStruct((feats * tiles, LANES), jnp.float32)
    return pl.pallas_call(
        kernel,
        grid=(width // step,),
        out_shape=[shape, shape],
        in_specs=[full(packed)]
        + [pl.BlockSpec((x.shape[0], step), lambda i: (0, i)) for x in pieces],
        out_specs=[pl.BlockSpec(shape.shape, lambda i: (0, 0))] * 2,
        scratch_shapes=[pltpu.VMEM((pairs, 2 * FEATS, 2 * span), jnp.bfloat16)],
        compiler_params=params(),
        cost_estimate=cost(4 * FEATS * 2 * span * pairs * width, 2 * 2 * span * pairs * width),
        name="gradients",
    )(packed, *pieces)


def body(cached_hidden, direction, expert_ids, gate_weights):
    rows = lax.axis_size("dp")
    experts = lax.axis_size("expert")
    span, width = cached_hidden.shape
    capacity = span // experts
    feats = direction.shape[1]
    scale = 1.0 / math.sqrt(expert_ids.shape[0] * rows * experts)
    steps = rows // 4
    ring = [(i, (i + 2) % rows if i % 2 == 0 else (i - 2) % rows) for i in range(rows)]
    partner = [(i, i ^ 1) for i in range(rows)]

    def shift(x):
        return lax.ppermute(x, "dp", ring)

    def swap(x):
        return lax.ppermute(x, "dp", partner)

    sent = message(cached_hidden, expert_ids, gate_weights, experts, capacity)
    other = swap(sent)
    chain_a = [shift(sent)]
    chain_b = [shift(other)]
    other_dir = swap(direction[0])
    pad = jnp.zeros((FEATS - feats, width), jnp.bfloat16)
    dirs = jnp.concatenate([direction[0], pad, other_dir, pad], axis=0)
    for _ in range(2, steps):
        chain_a.append(shift(chain_a[-1]))
        chain_b.append(shift(chain_b[-1]))
    last = shift(chain_a[-1])
    shape = (experts, 3 * steps, capacity, LANES)
    mix_shape = (2 * (steps - 1), span, 2 * span)
    kept = ()
    groups = []
    for s in range(1, steps):
        pieces = [chain_a[s - 1], chain_b[s - 1]]
        kept = tangents(s - 1, pieces, dirs, kept, shape, mix_shape, scale)
        groups.append(pieces)
    packed, mixes = kept
    own = own_tangents(cached_hidden, dirs)
    packed = last_tangents(steps - 1, own, last, dirs, packed)
    groups.append([cached_hidden, last])
    arrived = lax.all_to_all(packed, "expert", split_axis=0, concat_axis=0, tiled=True)
    adjoint = combine(arrived, mixes, [sent, last], scale)
    back = lax.all_to_all(adjoint, "expert", split_axis=0, concat_axis=0, tiled=True)
    mine, theirs = gradients(back, groups, feats)
    theirs = swap(theirs)
    return (mine + theirs).reshape(1, feats, width)


def solution(mesh):
    return jax.shard_map(
        body,
        mesh=mesh,
        in_specs=(
            P(("dp", "expert"), None),
            P("expert", "dp", None),
            P(("dp", "expert"), None),
            P(("dp", "expert"), None),
        ),
        out_specs=P("expert", "dp", None),
        check_vma=False,
    )
```

```python
import functools
import math

import jax
import jax.numpy as jnp
from jax import lax
from jax.experimental import pallas as pl
from jax.experimental.pallas import tpu as pltpu
from jax.sharding import PartitionSpec as P


VMEM = pltpu.VMEM
FEATS = 96
TAB = 8
LANES = 128
LIMIT = 24 * 2**20


def whole():
    return pl.BlockSpec(memory_space=VMEM)


def full(x):
    return pl.BlockSpec(x.shape, lambda i: (0,) * x.ndim)


def params():
    return pltpu.CompilerParams(vmem_limit_bytes=LIMIT)


def cost(flops, nbytes):
    return pl.CostEstimate(flops=flops, bytes_accessed=nbytes, transcendentals=0)


def message_kernel(capacity, experts, *refs):
    rows_hbm, ids_hbm, gates_hbm, dir_hbm, out_ref, head_ref, ids_ref, gates_ref, dir_ref, sems = refs
    topk, tokens = ids_ref.shape
    slots = experts * capacity
    span, width = rows_hbm.shape
    copies = [
        pltpu.make_async_copy(rows_hbm, out_ref.at[:span], sems.at[0]),
        pltpu.make_async_copy(ids_hbm, ids_ref, sems.at[1]),
        pltpu.make_async_copy(gates_hbm, gates_ref, sems.at[2]),
        pltpu.make_async_copy(rows_hbm.at[: head_ref.shape[0]], head_ref, sems.at[3]),
        pltpu.make_async_copy(dir_hbm, dir_ref, sems.at[4]),
    ]
    for copy in copies:
        copy.start()
    for copy in copies[1:3]:
        copy.wait()
    slot = lax.broadcasted_iota(jnp.int32, (slots, tokens), 0)
    expert = slot // capacity
    place = (slot % capacity).astype(jnp.float32)
    named = [ids_ref[k : k + 1, :] == expert for k in range(topk)]
    any_named = functools.reduce(jnp.logical_or, named)
    first = lax.broadcasted_iota(jnp.int32, (tokens, tokens), 0)
    second = lax.broadcasted_iota(jnp.int32, (tokens, tokens), 1)
    earlier = (first < second).astype(jnp.float32).astype(jnp.bfloat16)
    before = jnp.dot(
        any_named.astype(jnp.float32).astype(jnp.bfloat16),
        earlier,
        preferred_element_type=jnp.float32,
    )
    here = before == place
    token = lax.broadcasted_iota(jnp.int32, (1, tokens), 1).astype(jnp.float32)
    total = jnp.zeros((8, slots), jnp.float32)
    for k in range(topk):
        gate = gates_ref[k : k + 1, :]
        high = gate.astype(jnp.bfloat16).astype(jnp.float32)
        middle = (gate - high).astype(jnp.bfloat16).astype(jnp.float32)
        low = gate - high - middle
        rows = jnp.concatenate(
            [token, high, middle, low, jnp.zeros((4, tokens), jnp.float32)], axis=0
        ).astype(jnp.bfloat16)
        holds = jnp.logical_and(named[k], here).astype(jnp.float32).astype(jnp.bfloat16)
        total += lax.dot_general(
            rows, holds, (((1,), (1,)), ((), ())), preferred_element_type=jnp.float32
        )
    out_ref[span + FEATS :] = jnp.concatenate(
        [total, jnp.zeros((TAB, width - slots), jnp.float32)], axis=1
    ).astype(out_ref.dtype)
    feats = dir_ref.shape[0]
    copies[4].wait()
    out_ref[span : span + feats] = dir_ref[...]
    out_ref[span + feats : span + FEATS] = jnp.zeros((FEATS - feats, width), out_ref.dtype)
    copies[0].wait()
    copies[3].wait()


def message(rows, ids, gates, dirs, experts, capacity, cut):
    args = (rows, ids.T, gates.T, dirs)
    span, width = rows.shape
    return pl.pallas_call(
        functools.partial(message_kernel, capacity, experts),
        out_shape=[
            jax.ShapeDtypeStruct((span + TAB + FEATS, width), jnp.bfloat16),
            jax.ShapeDtypeStruct((cut, width), jnp.bfloat16),
        ],
        in_specs=[pl.BlockSpec(memory_space=pltpu.HBM)] * 4,
        out_specs=[whole(), whole()],
        scratch_shapes=[pltpu.VMEM(x.shape, x.dtype) for x in args[1:]]
        + [pltpu.SemaphoreType.DMA((5,))],
        cost_estimate=cost(10**7, 10**6),
        name="message",
    )(*args)


def split(sent, other, span, cut, join):
    width = sent.shape[1]
    left = span - cut
    sizes = (join + left + TAB, span - join + TAB, 2 * FEATS)

    def kernel(sent_ref, other_ref, first_ref, second_ref, dir_ref):
        first_ref[:join] = other_ref[:join]
        first_ref[join : join + left] = sent_ref[cut:span]
        first_ref[join + left :] = sent_ref[span + FEATS :]
        second_ref[: span - join] = other_ref[join:span]
        second_ref[span - join :] = other_ref[span + FEATS :]
        dir_ref[:FEATS] = sent_ref[span : span + FEATS]
        dir_ref[FEATS:] = other_ref[span : span + FEATS]

    return pl.pallas_call(
        kernel,
        out_shape=[jax.ShapeDtypeStruct((size, width), sent.dtype) for size in sizes],
        in_specs=[whole()] * 2,
        out_specs=[whole()] * 3,
        compiler_params=params(),
        cost_estimate=cost(0, 4 * sent.size),
        name="split",
    )(sent, other)


def table_of(rows):
    return pl.BlockSpec((TAB, LANES), lambda i: (rows.shape[0] // TAB - 1, 0))


def mix_of(table, scale):
    rows = table.astype(jnp.float32)
    slots = rows.shape[1]
    gate = rows[1:2] + rows[2:3] + rows[3:4]
    both = jnp.concatenate([rows[0:1], gate, jnp.zeros((6, slots), jnp.float32)], axis=0)
    columns = both.T
    mix = jnp.where(columns[:, 0:1] == both[0:1], (scale * columns[:, 1:2]) * both[1:2], 0.0)
    high = mix.astype(jnp.bfloat16)
    low = (mix - high.astype(jnp.float32)).astype(jnp.bfloat16)
    return jnp.concatenate([high, low], axis=1)


def project(rows, dirs):
    return lax.dot_general(
        rows, dirs, (((1,), (1,)), ((), ())), preferred_element_type=jnp.float32
    )


def pack(out_ref, values):
    sources = out_ref.shape[0]
    tail = jnp.concatenate([value[:, LANES:] for value in values], axis=1)
    for i, value in enumerate([value[:, :LANES] for value in values] + [tail]):
        out_ref[:, i] = value.reshape(sources, -1, LANES).astype(jnp.bfloat16)


def parts_of(span, cut, join):
    left = span - cut
    return ((0, 0, cut), (1, join, join + left), (1, 0, join), (2, 0, span - join))


def tangents(pair, pieces, parts, dirs, kept, shape, mix_shape, scale):
    sources, _, capacity, _ = shape
    span = sources * capacity
    args = list(pieces) + list(pieces[1:]) + [dirs] + list(kept)

    def kernel(*refs):
        dir_ref, out_ref, mix_ref = refs[5], refs[-2], refs[-1]
        rows = jnp.concatenate([refs[i][a:b, :] for i, a, b in parts], axis=0)
        value = project(rows, dir_ref[...])
        pack(out_ref, [value[:span], value[span:]])
        for i in range(2):
            mix_ref[i] = mix_of(refs[3 + i][...], scale)

    return pl.pallas_call(
        kernel,
        grid=(1,),
        out_shape=[
            jax.ShapeDtypeStruct(shape, jnp.bfloat16),
            jax.ShapeDtypeStruct(mix_shape, jnp.bfloat16),
        ],
        in_specs=[full(x) for x in pieces]
        + [table_of(x) for x in pieces[1:]]
        + [full(dirs)]
        + [pl.BlockSpec(memory_space=pl.ANY)] * len(kept),
        out_specs=[
            pl.BlockSpec((sources, 3, capacity, LANES), lambda i: (0, pair, 0, 0)),
            pl.BlockSpec((2,) + mix_shape[1:], lambda i: (pair, 0, 0)),
        ],
        input_output_aliases={6 + i: i for i in range(len(kept))},
        compiler_params=params(),
        cost_estimate=cost(4 * span * dirs.size, 2 * 2 * span * dirs.shape[1] + 2 * dirs.size),
        name="tangents",
    )(*args)


def own_tangents(rows, dirs):
    def kernel(rows_ref, dir_ref, out_ref):
        out_ref[...] = project(rows_ref[...], dir_ref[...])

    return pl.pallas_call(
        kernel,
        out_shape=jax.ShapeDtypeStruct((rows.shape[0], dirs.shape[0]), jnp.float32),
        in_specs=[whole(), whole()],
        out_specs=whole(),
        compiler_params=params(),
        cost_estimate=cost(2 * rows.shape[0] * dirs.size, 2 * rows.size + 2 * dirs.size),
        name="own_tangents",
    )(rows, dirs)


def last_tangents(pair, own, first, second, dirs, packed):
    sources, _, capacity, _ = packed.shape
    left = sources * capacity - first.shape[0]

    def kernel(own_ref, first_ref, second_ref, dir_ref, _, out_ref):
        rows = jnp.concatenate([first_ref[...], second_ref[:left, :]], axis=0)
        pack(out_ref, [own_ref[...], project(rows, dir_ref[...])])

    return pl.pallas_call(
        kernel,
        grid=(1,),
        out_shape=jax.ShapeDtypeStruct(packed.shape, packed.dtype),
        in_specs=[full(x) for x in (own, first, second, dirs)]
        + [pl.BlockSpec(memory_space=pl.ANY)],
        out_specs=pl.BlockSpec((sources, 3, capacity, LANES), lambda i: (0, pair, 0, 0)),
        input_output_aliases={4: 0},
        compiler_params=params(),
        cost_estimate=cost(2 * own.shape[0] * dirs.size, 2 * dirs.size),
        name="last_tangents",
    )(own, first, second, dirs, packed)


def combine(packed, mixes, tables, scale):
    experts, slabs, capacity, _ = packed.shape
    slots = experts * capacity

    def kernel(in_ref, mix_ref, *refs):
        out_ref = refs[-1]
        lane = lax.broadcasted_iota(jnp.int32, (slots, LANES), 1)

        def load(slab):
            return in_ref[:, slab].astype(jnp.float32).reshape(slots, LANES).astype(jnp.bfloat16)

        for pair in range(slabs // 3):
            tail = load(3 * pair + 2)
            tails = []
            for i in range(2):
                x = jnp.concatenate([load(3 * pair + i), tail], axis=1)
                here = 2 * pair + i
                if here < mixes.shape[0]:
                    mix = mix_ref[here]
                else:
                    mix = mix_of(refs[i][...], scale)
                y = jnp.dot(
                    mix, jnp.concatenate([x, x], axis=0), preferred_element_type=jnp.float32
                )
                tails.append(y[:, LANES:])
                out_ref[:, 3 * pair + i] = (
                    y[:, :LANES].reshape(experts, capacity, LANES).astype(jnp.bfloat16)
                )
            both = jnp.where(lane < LANES // 2, tails[0], tails[1])
            out_ref[:, 3 * pair + 2] = both.reshape(experts, capacity, LANES).astype(jnp.bfloat16)

    return pl.pallas_call(
        kernel,
        grid=(1,),
        out_shape=jax.ShapeDtypeStruct(packed.shape, packed.dtype),
        in_specs=[full(packed), full(mixes)] + [table_of(x) for x in tables],
        out_specs=full(packed),
        compiler_params=params(),
        cost_estimate=cost(10**9, 4 * packed.size),
        name="combine",
    )(packed, mixes, *tables)


def gradients(packed, groups, parts, feats):
    sources, slabs, capacity, _ = packed.shape
    span = sources * capacity
    pairs = slabs // 3
    width = groups[0][0].shape[1]
    tiles = width // LANES
    step = 2 * LANES
    pieces = [x for group in groups for x in group]

    def kernel(in_ref, *refs):
        own_ref, other_ref, lhs_ref = refs[-3:]
        column = pl.program_id(0)

        @pl.when(column == 0)
        def _():
            def turned(slab):
                rows = in_ref[:, slab].astype(jnp.float32).reshape(span, LANES)
                return rows.astype(jnp.bfloat16).T

            for pair in range(pairs):
                lhs_ref[pair, :LANES, :span] = turned(3 * pair)
                lhs_ref[pair, :LANES, span:] = turned(3 * pair + 1)
                tail = turned(3 * pair + 2)
                lhs_ref[pair, LANES:, :span] = tail[: LANES // 2]
                lhs_ref[pair, LANES:, span:] = tail[LANES // 2 :]

        total = None
        at = 0
        for pair in range(pairs):
            rows = [refs[at + i][a:b, :] for i, a, b in parts[pair]]
            at += len(groups[pair])
            term = jnp.dot(
                lhs_ref[pair], jnp.concatenate(rows, axis=0), preferred_element_type=jnp.float32
            )
            total = term if total is None else total + term
        for i in range(2):
            lanes = slice(i * LANES, (i + 1) * LANES)
            rows = pl.ds(2 * column + i, feats, stride=tiles)
            own_ref[rows, :] = total[:feats, lanes]
            other_ref[rows, :] = total[FEATS : FEATS + feats, lanes]

    shape = jax.ShapeDtypeStruct((feats * tiles, LANES), jnp.float32)
    return pl.pallas_call(
        kernel,
        grid=(width // step,),
        out_shape=[shape, shape],
        in_specs=[full(packed)]
        + [pl.BlockSpec((x.shape[0], step), lambda i: (0, i)) for x in pieces],
        out_specs=[pl.BlockSpec(shape.shape, lambda i: (0, 0))] * 2,
        scratch_shapes=[pltpu.VMEM((pairs, 2 * FEATS, 2 * span), jnp.bfloat16)],
        compiler_params=params(),
        cost_estimate=cost(4 * FEATS * 2 * span * pairs * width, 2 * 2 * span * pairs * width),
        name="gradients",
    )(packed, *pieces)


def body(cached_hidden, direction, expert_ids, gate_weights):
    rows = lax.axis_size("dp")
    experts = lax.axis_size("expert")
    span, width = cached_hidden.shape
    capacity = span // experts
    feats = direction.shape[1]
    scale = 1.0 / math.sqrt(expert_ids.shape[0] * rows * experts)
    steps = rows // 4
    ring = [(i, (i + 2) % rows if i % 2 == 0 else (i - 2) % rows) for i in range(rows)]
    partner = [(i, i ^ 1) for i in range(rows)]

    def shift(x):
        return lax.ppermute(x, "dp", ring)

    def swap(x):
        return lax.ppermute(x, "dp", partner)

    cut = span * 3 // 4
    join = span * 3 // 8
    parts = parts_of(span, cut, join)
    sent, head = message(
        cached_hidden, expert_ids, gate_weights, direction[0], experts, capacity, cut
    )
    other = swap(sent)
    middle, final, dirs = split(sent, other, span, cut, join)
    chain = [[shift(x)] for x in (head, middle, final)]
    for s in range(2, steps + 1):
        for k in range(3 if s < steps else 2):
            x = chain[k][-1]
            chain[k].append(shift(x[join:] if k == 1 and s == steps else x))
    last = [chain[0][-1], chain[1][-1]]
    shape = (experts, 3 * steps, capacity, LANES)
    mix_shape = (2 * (steps - 1), span, 2 * span)
    kept = ()
    groups = []
    for s in range(1, steps):
        pieces = [chain[k][s - 1] for k in range(3)]
        kept = tangents(s - 1, pieces, parts, dirs, kept, shape, mix_shape, scale)
        groups.append(pieces)
    packed, mixes = kept
    own = own_tangents(cached_hidden, dirs)
    packed = last_tangents(steps - 1, own, last[0], last[1], dirs, packed)
    groups.append([cached_hidden] + last)
    places = [parts] * (steps - 1) + [((0, 0, span), (1, 0, cut), (2, 0, span - cut))]
    arrived = lax.all_to_all(packed, "expert", split_axis=0, concat_axis=0, tiled=True)
    adjoint = combine(arrived, mixes, [middle, last[1]], scale)
    back = lax.all_to_all(adjoint, "expert", split_axis=0, concat_axis=0, tiled=True)
    mine, theirs = gradients(back, groups, places, feats)
    theirs = swap(theirs)
    return (mine + theirs).reshape(1, feats, width)


def solution(mesh):
    return jax.shard_map(
        body,
        mesh=mesh,
        in_specs=(
            P(("dp", "expert"), None),
            P("expert", "dp", None),
            P(("dp", "expert"), None),
            P(("dp", "expert"), None),
        ),
        out_specs=P("expert", "dp", None),
        check_vma=False,
    )
```

```python
import functools
import math

import jax
import jax.numpy as jnp
from jax import lax
from jax.experimental import pallas as pl
from jax.experimental.pallas import tpu as pltpu
from jax.sharding import PartitionSpec as P


VMEM = pltpu.VMEM
FEATS = 96
TAB = 8
LANES = 128
LIMIT = 24 * 2**20


def whole():
    return pl.BlockSpec(memory_space=VMEM)


def full(x):
    return pl.BlockSpec(x.shape, lambda i: (0,) * x.ndim)


def params():
    return pltpu.CompilerParams(vmem_limit_bytes=LIMIT)


def cost(flops, nbytes):
    return pl.CostEstimate(flops=flops, bytes_accessed=nbytes, transcendentals=0)


def message_kernel(capacity, experts, *refs):
    rows_hbm, ids_hbm, gates_hbm, dir_hbm, out_ref, head_ref, ids_ref, gates_ref, dir_ref, sems = refs
    topk, tokens = ids_ref.shape
    slots = experts * capacity
    span, width = rows_hbm.shape
    copies = [
        pltpu.make_async_copy(rows_hbm, out_ref.at[:span], sems.at[0]),
        pltpu.make_async_copy(ids_hbm, ids_ref, sems.at[1]),
        pltpu.make_async_copy(gates_hbm, gates_ref, sems.at[2]),
        pltpu.make_async_copy(rows_hbm.at[: head_ref.shape[0]], head_ref, sems.at[3]),
        pltpu.make_async_copy(dir_hbm, dir_ref, sems.at[4]),
    ]
    for copy in copies:
        copy.start()
    for copy in copies[1:3]:
        copy.wait()
    slot = lax.broadcasted_iota(jnp.int32, (slots, tokens), 0)
    expert = slot // capacity
    place = (slot % capacity).astype(jnp.float32)
    named = [ids_ref[k : k + 1, :] == expert for k in range(topk)]
    any_named = functools.reduce(jnp.logical_or, named)
    first = lax.broadcasted_iota(jnp.int32, (tokens, tokens), 0)
    second = lax.broadcasted_iota(jnp.int32, (tokens, tokens), 1)
    earlier = (first < second).astype(jnp.float32).astype(jnp.bfloat16)
    before = jnp.dot(
        any_named.astype(jnp.float32).astype(jnp.bfloat16),
        earlier,
        preferred_element_type=jnp.float32,
    )
    here = before == place
    token = lax.broadcasted_iota(jnp.int32, (1, tokens), 1).astype(jnp.float32)
    total = jnp.zeros((8, slots), jnp.float32)
    for k in range(topk):
        gate = gates_ref[k : k + 1, :]
        high = gate.astype(jnp.bfloat16).astype(jnp.float32)
        middle = (gate - high).astype(jnp.bfloat16).astype(jnp.float32)
        low = gate - high - middle
        rows = jnp.concatenate(
            [token, high, middle, low, jnp.zeros((4, tokens), jnp.float32)], axis=0
        ).astype(jnp.bfloat16)
        holds = jnp.logical_and(named[k], here).astype(jnp.float32).astype(jnp.bfloat16)
        total += lax.dot_general(
            rows, holds, (((1,), (1,)), ((), ())), preferred_element_type=jnp.float32
        )
    out_ref[span + FEATS :] = jnp.concatenate(
        [total, jnp.zeros((TAB, width - slots), jnp.float32)], axis=1
    ).astype(out_ref.dtype)
    feats = dir_ref.shape[0]
    copies[4].wait()
    out_ref[span : span + feats] = dir_ref[...]
    out_ref[span + feats : span + FEATS] = jnp.zeros((FEATS - feats, width), out_ref.dtype)
    copies[0].wait()
    copies[3].wait()


def message(rows, ids, gates, dirs, experts, capacity, cut):
    args = (rows, ids.T, gates.T, dirs)
    span, width = rows.shape
    return pl.pallas_call(
        functools.partial(message_kernel, capacity, experts),
        out_shape=[
            jax.ShapeDtypeStruct((span + TAB + FEATS, width), jnp.bfloat16),
            jax.ShapeDtypeStruct((cut, width), jnp.bfloat16),
        ],
        in_specs=[pl.BlockSpec(memory_space=pltpu.HBM)] * 4,
        out_specs=[whole(), whole()],
        scratch_shapes=[pltpu.VMEM(x.shape, x.dtype) for x in args[1:]]
        + [pltpu.SemaphoreType.DMA((5,))],
        cost_estimate=cost(10**7, 10**6),
        name="message",
    )(*args)


def split(sent, other, span, cut, join):
    width = sent.shape[1]
    left = span - cut
    sizes = (join + left + TAB, span - join, 2 * FEATS)

    def kernel(sent_ref, other_ref, first_ref, second_ref, dir_ref):
        first_ref[:join] = other_ref[:join]
        first_ref[join : join + left] = sent_ref[cut:span]
        first_ref[join + left :] = sent_ref[span + FEATS :]
        first_ref[join + left :, LANES : 2 * LANES] = other_ref[span + FEATS :, :LANES]
        second_ref[...] = other_ref[join:span]
        dir_ref[:FEATS] = sent_ref[span : span + FEATS]
        dir_ref[FEATS:] = other_ref[span : span + FEATS]

    return pl.pallas_call(
        kernel,
        out_shape=[jax.ShapeDtypeStruct((size, width), sent.dtype) for size in sizes],
        in_specs=[whole()] * 2,
        out_specs=[whole()] * 3,
        compiler_params=params(),
        cost_estimate=cost(0, 4 * sent.size),
        name="split",
    )(sent, other)


def table_of(rows, count=1):
    return pl.BlockSpec((TAB, count * LANES), lambda i: (rows.shape[0] // TAB - 1, 0))


def mix_of(table, scale):
    rows = table.astype(jnp.float32)
    slots = rows.shape[1]
    gate = rows[1:2] + rows[2:3] + rows[3:4]
    both = jnp.concatenate([rows[0:1], gate, jnp.zeros((6, slots), jnp.float32)], axis=0)
    columns = both.T
    mix = jnp.where(columns[:, 0:1] == both[0:1], (scale * columns[:, 1:2]) * both[1:2], 0.0)
    high = mix.astype(jnp.bfloat16)
    low = (mix - high.astype(jnp.float32)).astype(jnp.bfloat16)
    return jnp.concatenate([high, low], axis=1)


def project(rows, dirs):
    return lax.dot_general(
        rows, dirs, (((1,), (1,)), ((), ())), preferred_element_type=jnp.float32
    )


def pack(out_ref, values):
    sources = out_ref.shape[0]
    tail = jnp.concatenate([value[:, LANES:] for value in values], axis=1)
    for i, value in enumerate([value[:, :LANES] for value in values] + [tail]):
        out_ref[:, i] = value.reshape(sources, -1, LANES).astype(jnp.bfloat16)


def parts_of(span, cut, join):
    left = span - cut
    return ((0, 0, cut), (1, join, join + left), (1, 0, join), (2, 0, span - join))


def tangents(pair, pieces, parts, dirs, kept, shape, mix_shape, scale):
    sources, _, capacity, _ = shape
    span = sources * capacity
    args = list(pieces) + [pieces[1], dirs] + list(kept)

    def kernel(*refs):
        table_ref, dir_ref, out_ref, mix_ref = refs[3], refs[4], refs[-2], refs[-1]
        rows = jnp.concatenate([refs[i][a:b, :] for i, a, b in parts], axis=0)
        value = project(rows, dir_ref[...])
        pack(out_ref, [value[:span], value[span:]])
        for i in range(2):
            mix_ref[i] = mix_of(table_ref[:, i * LANES : (i + 1) * LANES], scale)

    return pl.pallas_call(
        kernel,
        grid=(1,),
        out_shape=[
            jax.ShapeDtypeStruct(shape, jnp.bfloat16),
            jax.ShapeDtypeStruct(mix_shape, jnp.bfloat16),
        ],
        in_specs=[full(x) for x in pieces]
        + [table_of(pieces[1], 2), full(dirs)]
        + [pl.BlockSpec(memory_space=pl.ANY)] * len(kept),
        out_specs=[
            pl.BlockSpec((sources, 3, capacity, LANES), lambda i: (0, pair, 0, 0)),
            pl.BlockSpec((2,) + mix_shape[1:], lambda i: (pair, 0, 0)),
        ],
        input_output_aliases={5 + i: i for i in range(len(kept))},
        compiler_params=params(),
        cost_estimate=cost(4 * span * dirs.size, 2 * 2 * span * dirs.shape[1] + 2 * dirs.size),
        name="tangents",
    )(*args)


def own_tangents(rows, dirs):
    def kernel(rows_ref, dir_ref, out_ref):
        out_ref[...] = project(rows_ref[...], dir_ref[...])

    return pl.pallas_call(
        kernel,
        out_shape=jax.ShapeDtypeStruct((rows.shape[0], dirs.shape[0]), jnp.float32),
        in_specs=[whole(), whole()],
        out_specs=whole(),
        compiler_params=params(),
        cost_estimate=cost(2 * rows.shape[0] * dirs.size, 2 * rows.size + 2 * dirs.size),
        name="own_tangents",
    )(rows, dirs)


def last_tangents(pair, own, first, second, dirs, packed):
    sources, _, capacity, _ = packed.shape
    left = sources * capacity - first.shape[0]

    def kernel(own_ref, first_ref, second_ref, dir_ref, _, out_ref):
        rows = jnp.concatenate([first_ref[...], second_ref[:left, :]], axis=0)
        pack(out_ref, [own_ref[...], project(rows, dir_ref[...])])

    return pl.pallas_call(
        kernel,
        grid=(1,),
        out_shape=jax.ShapeDtypeStruct(packed.shape, packed.dtype),
        in_specs=[full(x) for x in (own, first, second, dirs)]
        + [pl.BlockSpec(memory_space=pl.ANY)],
        out_specs=pl.BlockSpec((sources, 3, capacity, LANES), lambda i: (0, pair, 0, 0)),
        input_output_aliases={4: 0},
        compiler_params=params(),
        cost_estimate=cost(2 * own.shape[0] * dirs.size, 2 * dirs.size),
        name="last_tangents",
    )(own, first, second, dirs, packed)


def combine(packed, mixes, tables, scale):
    experts, slabs, capacity, _ = packed.shape
    slots = experts * capacity

    def kernel(in_ref, mix_ref, *refs):
        out_ref = refs[-1]
        lane = lax.broadcasted_iota(jnp.int32, (slots, LANES), 1)

        def load(slab):
            return in_ref[:, slab].astype(jnp.float32).reshape(slots, LANES).astype(jnp.bfloat16)

        for pair in range(slabs // 3):
            tail = load(3 * pair + 2)
            tails = []
            for i in range(2):
                x = jnp.concatenate([load(3 * pair + i), tail], axis=1)
                here = 2 * pair + i
                if here < mixes.shape[0]:
                    mix = mix_ref[here]
                else:
                    mix = mix_of(refs[i][...], scale)
                y = jnp.dot(
                    mix, jnp.concatenate([x, x], axis=0), preferred_element_type=jnp.float32
                )
                tails.append(y[:, LANES:])
                out_ref[:, 3 * pair + i] = (
                    y[:, :LANES].reshape(experts, capacity, LANES).astype(jnp.bfloat16)
                )
            both = jnp.where(lane < LANES // 2, tails[0], tails[1])
            out_ref[:, 3 * pair + 2] = both.reshape(experts, capacity, LANES).astype(jnp.bfloat16)

    return pl.pallas_call(
        kernel,
        grid=(1,),
        out_shape=jax.ShapeDtypeStruct(packed.shape, packed.dtype),
        in_specs=[full(packed), full(mixes)] + [table_of(x) for x in tables],
        out_specs=full(packed),
        compiler_params=params(),
        cost_estimate=cost(10**9, 4 * packed.size),
        name="combine",
    )(packed, mixes, *tables)


def gradients(packed, groups, parts, feats):
    sources, slabs, capacity, _ = packed.shape
    span = sources * capacity
    pairs = slabs // 3
    width = groups[0][0].shape[1]
    tiles = width // LANES
    step = 2 * LANES
    pieces = [x for group in groups for x in group]

    def kernel(in_ref, *refs):
        own_ref, other_ref, lhs_ref = refs[-3:]

        def turned(slab):
            rows = in_ref[:, slab].astype(jnp.float32).reshape(span, LANES)
            return rows.astype(jnp.bfloat16).T

        for pair in range(pairs):
            lhs_ref[pair, :LANES, :span] = turned(3 * pair)
            lhs_ref[pair, :LANES, span:] = turned(3 * pair + 1)
            tail = turned(3 * pair + 2)
            lhs_ref[pair, LANES:, :span] = tail[: LANES // 2]
            lhs_ref[pair, LANES:, span:] = tail[LANES // 2 :]
        for column in range(width // step):
            lanes = slice(column * step, (column + 1) * step)
            total = None
            at = 0
            for pair in range(pairs):
                rows = [refs[at + i][a:b, lanes] for i, a, b in parts[pair]]
                at += len(groups[pair])
                term = jnp.dot(
                    lhs_ref[pair], jnp.concatenate(rows, axis=0), preferred_element_type=jnp.float32
                )
                total = term if total is None else total + term
            for i in range(2):
                half = total[:, i * LANES : (i + 1) * LANES]
                rows = pl.ds(2 * column + i, feats, stride=tiles)
                own_ref[rows, :] = half[:feats]
                other_ref[rows, :] = half[FEATS : FEATS + feats]

    shape = jax.ShapeDtypeStruct((feats * tiles, LANES), jnp.float32)
    return pl.pallas_call(
        kernel,
        out_shape=[shape, shape],
        in_specs=[whole()] * (1 + len(pieces)),
        out_specs=[whole()] * 2,
        scratch_shapes=[pltpu.VMEM((pairs, 2 * FEATS, 2 * span), jnp.bfloat16)],
        compiler_params=params(),
        cost_estimate=cost(4 * FEATS * 2 * span * pairs * width, 2 * 2 * span * pairs * width),
        name="gradients",
    )(packed, *pieces)


def body(cached_hidden, direction, expert_ids, gate_weights):
    rows = lax.axis_size("dp")
    experts = lax.axis_size("expert")
    span, width = cached_hidden.shape
    capacity = span // experts
    feats = direction.shape[1]
    scale = 1.0 / math.sqrt(expert_ids.shape[0] * rows * experts)
    steps = rows // 4
    ring = [(i, (i + 2) % rows if i % 2 == 0 else (i - 2) % rows) for i in range(rows)]
    partner = [(i, i ^ 1) for i in range(rows)]

    def shift(x):
        return lax.ppermute(x, "dp", ring)

    def swap(x):
        return lax.ppermute(x, "dp", partner)

    cut = span * 3 // 4
    join = span * 3 // 8
    parts = parts_of(span, cut, join)
    sent, head = message(
        cached_hidden, expert_ids, gate_weights, direction[0], experts, capacity, cut
    )
    other = swap(sent)
    middle, final, dirs = split(sent, other, span, cut, join)
    chain = [[shift(x)] for x in (head, middle, final)]
    for s in range(2, steps + 1):
        for k in range(3 if s < steps else 2):
            x = chain[k][-1]
            chain[k].append(shift(x[join:] if k == 1 and s == steps else x))
    last = [chain[0][-1], chain[1][-1]]
    shape = (experts, 3 * steps, capacity, LANES)
    mix_shape = (2 * (steps - 1), span, 2 * span)
    kept = ()
    groups = []
    for s in range(1, steps):
        pieces = [chain[k][s - 1] for k in range(3)]
        kept = tangents(s - 1, pieces, parts, dirs, kept, shape, mix_shape, scale)
        groups.append(pieces)
    packed, mixes = kept
    own = own_tangents(cached_hidden, dirs)
    packed = last_tangents(steps - 1, own, last[0], last[1], dirs, packed)
    groups.append([cached_hidden] + last)
    places = [parts] * (steps - 1) + [((0, 0, span), (1, 0, cut), (2, 0, span - cut))]
    arrived = lax.all_to_all(packed, "expert", split_axis=0, concat_axis=0, tiled=True)
    adjoint = combine(arrived, mixes, [middle, last[1]], scale)
    back = lax.all_to_all(adjoint, "expert", split_axis=0, concat_axis=0, tiled=True)
    mine, theirs = gradients(back, groups, places, feats)
    theirs = swap(theirs)
    return (mine + theirs).reshape(1, feats, width)


def solution(mesh):
    return jax.shard_map(
        body,
        mesh=mesh,
        in_specs=(
            P(("dp", "expert"), None),
            P("expert", "dp", None),
            P(("dp", "expert"), None),
            P(("dp", "expert"), None),
        ),
        out_specs=P("expert", "dp", None),
        check_vma=False,
    )
```

```python
import functools
import math

import jax
import jax.numpy as jnp
from jax import lax
from jax.experimental import pallas as pl
from jax.experimental.pallas import tpu as pltpu
from jax.sharding import PartitionSpec as P


VMEM = pltpu.VMEM
FEATS = 96
TAB = 8
LANES = 128
LIMIT = 24 * 2**20


def whole():
    return pl.BlockSpec(memory_space=VMEM)


def full(x):
    return pl.BlockSpec(x.shape, lambda i: (0,) * x.ndim)


def params():
    return pltpu.CompilerParams(vmem_limit_bytes=LIMIT)


def cost(flops, nbytes):
    return pl.CostEstimate(flops=flops, bytes_accessed=nbytes, transcendentals=0)


def message_kernel(capacity, experts, *refs):
    rows_hbm, ids_hbm, gates_hbm, dir_hbm = refs[:4]
    out_ref, head_ref, keep_ref = refs[4:7]
    ids_ref, gates_ref, dir_ref, sems = refs[7:]
    topk, tokens = ids_ref.shape
    slots = experts * capacity
    span, width = rows_hbm.shape
    copies = [
        pltpu.make_async_copy(rows_hbm, out_ref.at[:span], sems.at[0]),
        pltpu.make_async_copy(ids_hbm, ids_ref, sems.at[1]),
        pltpu.make_async_copy(gates_hbm, gates_ref, sems.at[2]),
        pltpu.make_async_copy(rows_hbm.at[: head_ref.shape[0]], head_ref, sems.at[3]),
        pltpu.make_async_copy(dir_hbm, dir_ref, sems.at[4]),
    ]
    for copy in copies:
        copy.start()
    for copy in copies[1:3]:
        copy.wait()
    slot = lax.broadcasted_iota(jnp.int32, (slots, tokens), 0)
    expert = slot // capacity
    place = (slot % capacity).astype(jnp.float32)
    named = [ids_ref[k : k + 1, :] == expert for k in range(topk)]
    any_named = functools.reduce(jnp.logical_or, named)
    first = lax.broadcasted_iota(jnp.int32, (tokens, tokens), 0)
    second = lax.broadcasted_iota(jnp.int32, (tokens, tokens), 1)
    earlier = (first < second).astype(jnp.float32).astype(jnp.bfloat16)
    before = jnp.dot(
        any_named.astype(jnp.float32).astype(jnp.bfloat16),
        earlier,
        preferred_element_type=jnp.float32,
    )
    here = before == place
    token = lax.broadcasted_iota(jnp.int32, (1, tokens), 1).astype(jnp.float32)
    total = jnp.zeros((8, slots), jnp.float32)
    for k in range(topk):
        gate = gates_ref[k : k + 1, :]
        high = gate.astype(jnp.bfloat16).astype(jnp.float32)
        middle = (gate - high).astype(jnp.bfloat16).astype(jnp.float32)
        low = gate - high - middle
        rows = jnp.concatenate(
            [token, high, middle, low, jnp.zeros((4, tokens), jnp.float32)], axis=0
        ).astype(jnp.bfloat16)
        holds = jnp.logical_and(named[k], here).astype(jnp.float32).astype(jnp.bfloat16)
        total += lax.dot_general(
            rows, holds, (((1,), (1,)), ((), ())), preferred_element_type=jnp.float32
        )
    out_ref[span + FEATS :] = jnp.concatenate(
        [total, jnp.zeros((TAB, width - slots), jnp.float32)], axis=1
    ).astype(out_ref.dtype)
    feats = dir_ref.shape[0]
    copies[4].wait()
    out_ref[span : span + feats] = dir_ref[...]
    out_ref[span + feats : span + FEATS] = jnp.zeros((FEATS - feats, width), out_ref.dtype)
    copies[0].wait()
    cut = head_ref.shape[0]
    keep_ref[...] = out_ref[cut:]
    copies[3].wait()


def message(rows, ids, gates, dirs, experts, capacity, cut):
    args = (rows, ids.T, gates.T, dirs)
    span, width = rows.shape
    return pl.pallas_call(
        functools.partial(message_kernel, capacity, experts),
        out_shape=[
            jax.ShapeDtypeStruct((span + TAB + FEATS, width), jnp.bfloat16),
            jax.ShapeDtypeStruct((cut, width), jnp.bfloat16),
            pltpu.VMEM((span - cut + FEATS + TAB, width), jnp.bfloat16),
        ],
        in_specs=[pl.BlockSpec(memory_space=pltpu.HBM)] * 4,
        out_specs=[whole()] * 3,
        scratch_shapes=[pltpu.VMEM(x.shape, x.dtype) for x in args[1:]]
        + [pltpu.SemaphoreType.DMA((5,))],
        cost_estimate=cost(10**7, 10**6),
        name="message",
    )(*args)


def split(keep, other, span, cut, join):
    width = keep.shape[1]
    left = span - cut
    sizes = (join + left + TAB, span - join, 2 * FEATS)

    def kernel(keep_ref, other_ref, first_ref, second_ref, dir_ref):
        first_ref[:join] = other_ref[:join]
        first_ref[join : join + left] = keep_ref[:left]
        first_ref[join + left :] = keep_ref[left + FEATS :]
        first_ref[join + left :, LANES : 2 * LANES] = other_ref[span + FEATS :, :LANES]
        second_ref[...] = other_ref[join:span]
        dir_ref[:FEATS] = keep_ref[left : left + FEATS]
        dir_ref[FEATS:] = other_ref[span : span + FEATS]

    return pl.pallas_call(
        kernel,
        out_shape=[jax.ShapeDtypeStruct((size, width), keep.dtype) for size in sizes],
        in_specs=[whole()] * 2,
        out_specs=[whole()] * 3,
        compiler_params=params(),
        cost_estimate=cost(0, 4 * other.size),
        name="split",
    )(keep, other)


def table_of(rows, count=1):
    return pl.BlockSpec((TAB, count * LANES), lambda i: (rows.shape[0] // TAB - 1, 0))


def mix_of(table, scale):
    rows = table.astype(jnp.float32)
    slots = rows.shape[1]
    gate = rows[1:2] + rows[2:3] + rows[3:4]
    both = jnp.concatenate([rows[0:1], gate, jnp.zeros((6, slots), jnp.float32)], axis=0)
    columns = both.T
    mix = jnp.where(columns[:, 0:1] == both[0:1], (scale * columns[:, 1:2]) * both[1:2], 0.0)
    high = mix.astype(jnp.bfloat16)
    low = (mix - high.astype(jnp.float32)).astype(jnp.bfloat16)
    return jnp.concatenate([high, low], axis=1)


def project(rows, dirs):
    return lax.dot_general(
        rows, dirs, (((1,), (1,)), ((), ())), preferred_element_type=jnp.float32
    )


def pack(out_ref, values):
    sources = out_ref.shape[0]
    tail = jnp.concatenate([value[:, LANES:] for value in values], axis=1)
    for i, value in enumerate([value[:, :LANES] for value in values] + [tail]):
        out_ref[:, i] = value.reshape(sources, -1, LANES).astype(jnp.bfloat16)


def parts_of(span, cut, join):
    left = span - cut
    return ((0, 0, cut), (1, join, join + left), (1, 0, join), (2, 0, span - join))


def tangents(pair, pieces, parts, dirs, kept, shape, mix_shape, scale):
    sources, _, capacity, _ = shape
    span = sources * capacity
    args = list(pieces) + [pieces[1], dirs] + list(kept)

    def kernel(*refs):
        table_ref, dir_ref, out_ref, mix_ref = refs[3], refs[4], refs[-2], refs[-1]
        rows = jnp.concatenate([refs[i][a:b, :] for i, a, b in parts], axis=0)
        value = project(rows, dir_ref[...])
        pack(out_ref, [value[:span], value[span:]])
        for i in range(2):
            mix_ref[i] = mix_of(table_ref[:, i * LANES : (i + 1) * LANES], scale)

    return pl.pallas_call(
        kernel,
        grid=(1,),
        out_shape=[
            jax.ShapeDtypeStruct(shape, jnp.bfloat16),
            jax.ShapeDtypeStruct(mix_shape, jnp.bfloat16),
        ],
        in_specs=[full(x) for x in pieces]
        + [table_of(pieces[1], 2), full(dirs)]
        + [pl.BlockSpec(memory_space=pl.ANY)] * len(kept),
        out_specs=[
            pl.BlockSpec((sources, 3, capacity, LANES), lambda i: (0, pair, 0, 0)),
            pl.BlockSpec((2,) + mix_shape[1:], lambda i: (pair, 0, 0)),
        ],
        input_output_aliases={5 + i: i for i in range(len(kept))},
        compiler_params=params(),
        cost_estimate=cost(4 * span * dirs.size, 2 * 2 * span * dirs.shape[1] + 2 * dirs.size),
        name="tangents",
    )(*args)


def own_tangents(rows, dirs):
    def kernel(rows_ref, dir_ref, out_ref):
        out_ref[...] = project(rows_ref[...], dir_ref[...])

    return pl.pallas_call(
        kernel,
        out_shape=jax.ShapeDtypeStruct((rows.shape[0], dirs.shape[0]), jnp.float32),
        in_specs=[whole(), whole()],
        out_specs=whole(),
        compiler_params=params(),
        cost_estimate=cost(2 * rows.shape[0] * dirs.size, 2 * rows.size + 2 * dirs.size),
        name="own_tangents",
    )(rows, dirs)


def last_tangents(pair, own, first, second, dirs, packed):
    sources, _, capacity, _ = packed.shape
    left = sources * capacity - first.shape[0]

    def kernel(own_ref, first_ref, second_ref, dir_ref, _, out_ref):
        rows = jnp.concatenate([first_ref[...], second_ref[:left, :]], axis=0)
        pack(out_ref, [own_ref[...], project(rows, dir_ref[...])])

    return pl.pallas_call(
        kernel,
        grid=(1,),
        out_shape=jax.ShapeDtypeStruct(packed.shape, packed.dtype),
        in_specs=[full(x) for x in (own, first, second, dirs)]
        + [pl.BlockSpec(memory_space=pl.ANY)],
        out_specs=pl.BlockSpec((sources, 3, capacity, LANES), lambda i: (0, pair, 0, 0)),
        input_output_aliases={4: 0},
        compiler_params=params(),
        cost_estimate=cost(2 * own.shape[0] * dirs.size, 2 * dirs.size),
        name="last_tangents",
    )(own, first, second, dirs, packed)


def combine(packed, mixes, tables, scale):
    experts, slabs, capacity, _ = packed.shape
    slots = experts * capacity

    def kernel(in_ref, mix_ref, *refs):
        out_ref = refs[-1]
        lane = lax.broadcasted_iota(jnp.int32, (slots, LANES), 1)

        def load(slab):
            return in_ref[:, slab].astype(jnp.float32).reshape(slots, LANES).astype(jnp.bfloat16)

        for pair in range(slabs // 3):
            tail = load(3 * pair + 2)
            tails = []
            for i in range(2):
                x = jnp.concatenate([load(3 * pair + i), tail], axis=1)
                here = 2 * pair + i
                if here < mixes.shape[0]:
                    mix = mix_ref[here]
                else:
                    mix = mix_of(refs[i][...], scale)
                y = jnp.dot(
                    mix, jnp.concatenate([x, x], axis=0), preferred_element_type=jnp.float32
                )
                tails.append(y[:, LANES:])
                out_ref[:, 3 * pair + i] = (
                    y[:, :LANES].reshape(experts, capacity, LANES).astype(jnp.bfloat16)
                )
            both = jnp.where(lane < LANES // 2, tails[0], tails[1])
            out_ref[:, 3 * pair + 2] = both.reshape(experts, capacity, LANES).astype(jnp.bfloat16)

    return pl.pallas_call(
        kernel,
        grid=(1,),
        out_shape=jax.ShapeDtypeStruct(packed.shape, packed.dtype),
        in_specs=[full(packed), full(mixes)] + [table_of(x) for x in tables],
        out_specs=full(packed),
        compiler_params=params(),
        cost_estimate=cost(10**9, 4 * packed.size),
        name="combine",
    )(packed, mixes, *tables)


def gradients(packed, groups, parts, feats, first):
    sources, slabs, capacity, _ = packed.shape
    span = sources * capacity
    pairs = slabs // 3
    width = groups[0][0].shape[1]
    tiles = width // LANES
    step = 2 * LANES
    half = LANES // 2
    pieces = [x for group in groups for x in group]

    def kernel(in_ref, *refs):
        out_ref, lhs_ref = refs[-2:]

        def turned(slab):
            rows = in_ref[:, slab].astype(jnp.float32).reshape(span, LANES)
            return rows.astype(jnp.bfloat16).T

        for pair in range(pairs):
            for i in range(2):
                columns = slice(i * span, (i + 1) * span)
                main = turned(3 * pair + i)
                if first:
                    lhs_ref[pair, :, columns] = main[:FEATS]
                else:
                    lhs_ref[pair, : LANES - FEATS, columns] = main[FEATS:]
            if not first:
                tail = turned(3 * pair + 2)
                lhs_ref[pair, LANES - FEATS :, :span] = tail[:half]
                lhs_ref[pair, LANES - FEATS :, span:] = tail[half:]
        for column in range(width // step):
            lanes = slice(column * step, (column + 1) * step)
            total = None
            at = 0
            for pair in range(pairs):
                rows = [refs[at + i][a:b, lanes] for i, a, b in parts[pair]]
                at += len(groups[pair])
                term = jnp.dot(
                    lhs_ref[pair], jnp.concatenate(rows, axis=0), preferred_element_type=jnp.float32
                )
                total = term if total is None else total + term
            for i in range(2):
                rows = pl.ds(2 * column + i, feats, stride=tiles)
                out_ref[rows, :] = total[:feats, i * LANES : (i + 1) * LANES]

    return pl.pallas_call(
        kernel,
        out_shape=jax.ShapeDtypeStruct((feats * tiles, LANES), jnp.float32),
        in_specs=[whole()] * (1 + len(pieces)),
        out_specs=whole(),
        scratch_shapes=[pltpu.VMEM((pairs, FEATS, 2 * span), jnp.bfloat16)],
        compiler_params=params(),
        cost_estimate=cost(2 * FEATS * 2 * span * pairs * width, 2 * 2 * span * pairs * width),
        name="gradients",
    )(packed, *pieces)


def body(cached_hidden, direction, expert_ids, gate_weights):
    rows = lax.axis_size("dp")
    experts = lax.axis_size("expert")
    span, width = cached_hidden.shape
    capacity = span // experts
    feats = direction.shape[1]
    scale = 1.0 / math.sqrt(expert_ids.shape[0] * rows * experts)
    steps = rows // 4
    ring = [(i, (i + 2) % rows if i % 2 == 0 else (i - 2) % rows) for i in range(rows)]
    partner = [(i, i ^ 1) for i in range(rows)]

    def shift(x):
        return lax.ppermute(x, "dp", ring)

    def swap(x):
        return lax.ppermute(x, "dp", partner)

    cut = span * 3 // 4
    join = span * 3 // 8
    parts = parts_of(span, cut, join)
    sent, head, keep = message(
        cached_hidden, expert_ids, gate_weights, direction[0], experts, capacity, cut
    )
    other = swap(sent)
    middle, final, dirs = split(keep, other, span, cut, join)
    chain = [[shift(x)] for x in (head, middle, final)]
    for s in range(2, steps + 1):
        for k in range(3 if s < steps else 2):
            x = chain[k][-1]
            chain[k].append(shift(x[join:] if k == 1 and s == steps else x))
    last = [chain[0][-1], chain[1][-1]]
    shape = (experts, 3 * steps, capacity, LANES)
    mix_shape = (2 * (steps - 1), span, 2 * span)
    kept = ()
    groups = []
    for s in range(1, steps):
        pieces = [chain[k][s - 1] for k in range(3)]
        kept = tangents(s - 1, pieces, parts, dirs, kept, shape, mix_shape, scale)
        groups.append(pieces)
    packed, mixes = kept
    own = own_tangents(cached_hidden, dirs)
    packed = last_tangents(steps - 1, own, last[0], last[1], dirs, packed)
    groups.append([cached_hidden] + last)
    places = [parts] * (steps - 1) + [((0, 0, span), (1, 0, cut), (2, 0, span - cut))]
    arrived = lax.all_to_all(packed, "expert", split_axis=0, concat_axis=0, tiled=True)
    adjoint = combine(arrived, mixes, [middle, last[1]], scale)
    back = lax.all_to_all(adjoint, "expert", split_axis=0, concat_axis=0, tiled=True)
    theirs = gradients(back, groups, places, feats, False)
    mine = gradients(back, groups, places, feats, True)
    theirs = swap(theirs)
    return (mine + theirs).reshape(1, feats, width)


def solution(mesh):
    return jax.shard_map(
        body,
        mesh=mesh,
        in_specs=(
            P(("dp", "expert"), None),
            P("expert", "dp", None),
            P(("dp", "expert"), None),
            P(("dp", "expert"), None),
        ),
        out_specs=P("expert", "dp", None),
        check_vma=False,
    )
```
